128 devices in a mesh: blk: 16 (over y_hi, x, core), rep: 8 (over z, y_lo).
Axes of the slice: x: 4, y: 4 (y_hi: 2, y_lo: 2; y = y_hi * 2 + y_lo), z: 4, core: 2. Of those that a mesh axis runs over, the one named last changes fastest.
Arguments:
- p_tiles: float32 [16, 8, 8, 5, 128, 128], P('blk', 'rep'), may hold values from -1 to 1
- tasks: int32 [16, 8, 8, 3, 48], P('blk', 'rep'), may hold values from 0 to 39, as said below
Outputs:
- density_square: float32 [16, 8, 16, 128, 128], P('blk', 'rep')
The draws below stay inside these ranges and needn't reach their ends.
Inputs may be any that keep to these rules, and one draw needn't show every extreme that they name: Row 0 of tasks[b, r, s] indexes the 40 tiles of left_s, row 1 the 40 tiles of right_s, row 2 the target tile, where 16 marks an unused slot. Used slots come first in each list; each list has 12 to 48 used slots, and some list has all 48.
All inputs are finite; a program needn't handle non-finite values.
Results may differ from the reference program's by a relative error of at most 0.0003.
Values sent between devices are 32-bit elements; how exact they have to be, the bound alone decides.
A program may use at most 192 MiB of HBM per device.

```python
import jax
import jax.numpy as jnp
from jax import lax

TILE = 128
TPS = 5
NTASK = 48
NC = 16
PANELS = 16
SLIVERS = 8
RSTEPS = 8
NT = 40
GROUP_TILES = 40


def draw_tasks(key, part):
    keys = jax.random.split(jax.random.fold_in(key, 17), 5)
    lists = (PANELS, SLIVERS, RSTEPS)
    shape = (PANELS, SLIVERS, RSTEPS, NTASK)
    lowest = NTASK // 4
    span = NTASK - lowest + 1
    raw = jax.random.randint(keys[0], lists, 0, span)
    live = lowest + raw * raw // span
    spot = jax.random.randint(keys[1], (), 0, PANELS * SLIVERS * RSTEPS)
    flat = live.reshape(-1)
    flat = jnp.where(jnp.arange(flat.shape[0]) == spot, NTASK, flat)
    live = flat.reshape(lists)
    first = jax.random.randint(keys[2], shape, 0, GROUP_TILES)
    second = jax.random.randint(keys[3], shape, 0, NT)
    target = jax.random.randint(keys[4], shape, 0, NC)
    slots = jnp.arange(NTASK)
    target = jnp.where(slots < live[..., None], target, NC)
    return jnp.stack([first, second, target], axis=3).astype(jnp.int32)


def levels(own_key, extent, shards, low, top_value):
    def one(position, shards_of):
        heights = jax.random.uniform(jax.random.fold_in(jax.random.fold_in(own_key, 6), position), (shards_of,), jnp.float32, low / len(shards), top_value / len(shards))
        return jnp.repeat(jnp.exp(heights), extent[position] // shards_of).reshape((-1,) + (1,) * (len(extent) - position - 1))

    factor_of = one(*shards[0])
    for cut in shards[1:]:
        factor_of = factor_of * one(*cut)
    return factor_of


def bell_draw(rng, shape, scale, most, pieces=(), kind=jnp.bfloat16):
    array = scale * jax.random.normal(rng, shape, jnp.float32)
    if pieces:
        array = array * levels(rng, shape, pieces, -0.22, 0.18)
    return jnp.clip(array, -most, most).astype(kind)


def setup_inputs(seed: int = 0) -> dict:
    splits = jax.random.split(jax.random.key(seed), 3)
    return {
        "p_tiles": bell_draw(splits[0], (PANELS, SLIVERS, RSTEPS, TPS, TILE, TILE), 0.18, 1.0, ((0, 16), (1, 8)), jnp.float32),
        "tasks": draw_tasks(jax.random.fold_in(splits[2], 71), 0),
    }


def reference(p_tiles, tasks):
    def one_device(index):
        panel_index = index // SLIVERS
        sliver_index = index % SLIVERS
        task_list = tasks[panel_index, sliver_index]
        summed = jnp.zeros((NC + 1, TILE, TILE), p_tiles.dtype)
        for step in range(RSTEPS):
            left_tiles = p_tiles[panel_index, :, step].reshape(GROUP_TILES, TILE, TILE)
            source = ((panel_index - step) % PANELS).astype(jnp.int32)
            right_tiles = p_tiles[source, sliver_index].reshape(NT, TILE, TILE)
            left_pick = left_tiles[task_list[step, 0]]
            right_pick = right_tiles[task_list[step, 1]]
            product = jnp.einsum("nij,njk->nik", left_pick, right_pick, precision=lax.Precision.HIGHEST)
            summed = summed + jax.ops.segment_sum(product, task_list[step, 2], num_segments=NC + 1)
        return summed[:NC]

    result = lax.map(one_device, jnp.arange(PANELS * SLIVERS, dtype=jnp.int32))
    return result.reshape(PANELS, SLIVERS, NC, TILE, TILE)
```

```python
import jax
import jax.numpy as jnp
from jax import lax
from jax.experimental import pallas as pl
from jax.experimental.pallas import tpu as pltpu
from jax.sharding import PartitionSpec as P

MESH = pl.DeviceIdType.MESH
TILE = 128
NT = 40
TPS = 5
NC = 16
NTASK = 48
CH = 10
NCH = NT // CH
ORDER_OF_CHUNK = (0, 1, 3, 2)


def sort_tasks(tasks):
    left, right, target = tasks[:, 0], tasks[:, 1], tasks[:, 2]
    slots = jnp.arange(NTASK, dtype=jnp.int32)
    before = (target[:, None, :] < target[:, :, None]) | (
        (target[:, None, :] == target[:, :, None]) & (slots[None, None, :] < slots[None, :, None])
    )
    rank = jnp.sum(before.astype(jnp.int32), axis=2)
    place = (rank[:, :, None] == slots[None, None, :]).astype(jnp.int32)
    pick = lambda v: jnp.sum(place * v[:, :, None], axis=1)
    sorted_target = pick(target)
    same = jnp.concatenate(
        [jnp.zeros_like(target[:, :1]), (sorted_target[:, 1:] == sorted_target[:, :-1]).astype(jnp.int32)], axis=1
    )
    cols = jnp.arange(NC, dtype=jnp.int32)
    count = jnp.sum((target[:, :, None] == cols).astype(jnp.int32), axis=1)
    upto = jnp.sum((target[:, :, None] <= cols).astype(jnp.int32), axis=1)
    last = jnp.maximum(upto - 1, 0)
    wide = lambda v: jnp.pad(v, ((0, 0), (0, 128 - v.shape[1])))
    rows = [wide(jnp.clip(pick(left), 0, NT - 1)), wide(jnp.clip(pick(right), 0, NT - 1)), wide(same), wide(last)]
    rows.append(wide((count > 0).astype(jnp.int32)))
    rows += [jnp.zeros_like(rows[0])] * 3
    return jnp.stack(rows, axis=1)


def kernel(p_ref, meta_ref, out_ref, *scratch):
    lefts = scratch[0:4]
    rights = (scratch[4:6], scratch[6:8], scratch[8:10], scratch[10:12])
    four = scratch[12:14]
    (five, sums, partial, arrived, meta_in, meta_sm) = scratch[14:20]
    (ry, rplus, rminus, rcross, rz, rd, rmeta, rc) = scratch[20:28]
    (sy, splus, sminus, scross, sz, sd, smeta, sc) = scratch[28:36]
    (l_own, l_left, l_part, l_meta) = scratch[36:40]

    blk, rep = lax.axis_index("blk"), lax.axis_index("rep")
    h, x, k = blk // 8, (blk % 8) // 2, blk % 2
    z, lo = rep // 2, rep % 2
    p = (lo + h) % 2
    holder = k == p
    mate = rep + 1 - 2 * lo
    at_plus = (h * 8 + ((x + 1) % 4) * 2 + k, rep)
    at_minus = (h * 8 + ((x + 3) % 4) * 2 + k, rep)
    at_mate = (blk, mate)
    at_cross = ((1 - h) * 8 + x * 2 + k, mate)
    at_zp = (blk, ((z + 1) % 4) * 2 + lo)
    at_zm = (blk, ((z + 3) % 4) * 2 + lo)
    at_sib = (blk + 1 - 2 * k, rep)

    def s_of(n, parity):
        odd = (k + parity) % 2
        f = (1 - k) * parity
        return odd + (0, 2, 6, 4)[n] + f * (0, 4, -2, -2)[n]

    barrier = pltpu.get_barrier_semaphore()
    for peer in (at_plus, at_minus, at_mate, at_cross, at_zp, at_zm, at_sib):
        pl.semaphore_signal(barrier, inc=1, device_id=peer, device_id_type=MESH)
    pl.semaphore_wait(barrier, 7)

    def remote(src, dst, ssem, rsem, peer):
        return pltpu.make_async_remote_copy(
            src_ref=src, dst_ref=dst, send_sem=ssem, recv_sem=rsem, device_id=peer, device_id_type=MESH
        )

    def rows(ref, i):
        return ref.at[pl.ds(CH * i, CH)]

    def five_of(ref, r):
        return ref.at[pl.ds(TPS * r, TPS)]

    def landed(ref, sem):
        pltpu.make_async_copy(ref, ref, sem).wait()

    def to_plus(src, dst, i, slot):
        remote(src, rows(dst, i), splus.at[slot], rplus.at[slot], at_plus).start()

    def to_minus(src, dst, i, slot):
        remote(src, rows(dst, i), sminus.at[slot], rminus.at[slot], at_minus).start()

    def to_cross(src, dst, i, slot):
        remote(src, rows(dst, i), scross.at[slot], rcross.at[slot], at_cross).start()

    def to_sibling(src, n, q, i):
        remote(src, rows(rights[n][q], i), sd.at[2 * n + q], rd.at[2 * n + q], at_sib).start()

    def z_both(src, n, r, kind):
        dst = five_of(lefts[n], r)
        remote(src, dst, sz.at[0, kind, n], rz.at[0, kind, n], at_zp).start()
        remote(src, dst, sz.at[1, kind, n], rz.at[1, kind, n], at_zm).start()

    def own_left(n):
        return p_ref.at[pl.ds(TPS * s_of(n, p), TPS)]

    def start():
        @pl.when(holder)
        def _():
            for n in range(4):
                src = p_ref.at[pl.ds(TPS * s_of(n, 1 - p), TPS)]
                remote(src, five_of(lefts[n], rep), sy.at[n], ry.at[n], at_mate).start()
            for i in range(NCH):
                src = rows(p_ref, i)

                @pl.when(x != 3)
                def _():
                    to_plus(src, rights[1][0], i, i)

                @pl.when(x == 0)
                def _():
                    to_minus(src, rights[2][0], i, i)

                to_cross(src, four[1], i, NCH + i)

            @pl.when(p == 0)
            def _():
                remote(p_ref, rights[0][0], sd.at[0], rd.at[0], at_sib).start()

            pltpu.make_async_copy(p_ref, rights[0][0], l_own).start()

        @pl.when(jnp.logical_not(holder))
        def _():
            for i in range(NCH):
                remote(rows(p_ref, i), rows(rights[0][1], i), sy.at[i], ry.at[i], at_mate).start()

        for n in range(4):
            pltpu.make_async_copy(own_left(n), five_of(lefts[n], rep), l_left.at[n]).start()
        for n in range(2):
            z_both(own_left(n), n, rep, 0)
        for n in range(4):
            remote(meta_ref.at[s_of(n, 1 - p)], meta_in.at[n], smeta.at[n], rmeta.at[n], at_mate).start()
            pltpu.make_async_copy(meta_ref.at[s_of(n, p)], meta_sm.at[0, n], l_meta.at[0, n]).start()

    def on_meta():
        for n in range(4):
            landed(meta_in.at[n], rmeta.at[n])
            pltpu.make_async_copy(meta_in.at[n], meta_sm.at[1, n], l_meta.at[1, n]).start()
        for q in range(2):
            for n in range(4):
                landed(meta_sm.at[q, n], l_meta.at[q, n])

    def on_mate(i):
        @pl.when(holder)
        def _():
            n = ORDER_OF_CHUNK[i]
            src = rows(rights[0][1], i)
            landed(src, ry.at[i])
            head = rights[0][1].at[pl.ds(CH * i, TPS)]
            z_both(head, n, mate, 1)
            pltpu.make_async_copy(head, five_of(lefts[n], mate), l_part.at[n]).start()

            @pl.when(x != 3)
            def _():
                to_plus(src, rights[1][1], i, NCH + i)

            @pl.when(x == 0)
            def _():
                to_minus(src, rights[2][1], i, NCH + i)

            to_cross(src, four[0], i, i)

            @pl.when(p == 0)
            def _():
                to_sibling(src, 0, 1, i)

        @pl.when(jnp.logical_not(holder))
        def _():
            src = five_of(lefts[i], mate)
            landed(src, ry.at[i])
            z_both(src, i, mate, 1)

    def send_own_left(n):
        z_both(own_left(n), n, rep, 0)

    def on_z(kind, n):
        for side in range(2):
            away = (z + 3) % 4 if side == 0 else (z + 1) % 4
            if kind == 2:
                away = (z + 2) % 4
            own_side = kind == 0 or (kind == 2 and side == 0)
            r = away * 2 + (lo if own_side else 1 - lo)
            src = five_of(lefts[n], r)
            landed(src, rz.at[side, kind, n])
            if kind == 0 and side == 0:
                remote(src, src, sz.at[0, 2, n], rz.at[0, 2, n], at_zp).start()
            if kind == 1 and side == 1:
                remote(src, src, sz.at[1, 2, n], rz.at[1, 2, n], at_zm).start()

    def on_cross(q, i):
        @pl.when(holder)
        def _():
            src = rows(four[q], i)
            landed(src, rcross.at[q * NCH + i])

            @pl.when(x == 3)
            def _():
                to_plus(src, rights[1][q], i, q * NCH + i)

            @pl.when(x != 0)
            def _():
                to_minus(src, rights[2][q], i, q * NCH + i)

            @pl.when(p == 1)
            def _():
                to_sibling(src, 1, q, i)

    def on_plus_of(q, i, here):
        @pl.when(jnp.logical_and(holder, here))
        def _():
            src = rows(rights[1][q], i)
            landed(src, rplus.at[q * NCH + i])
            if q == 0:

                @pl.when(x != 3)
                def _():
                    to_plus(src, rights[3][0], i, 2 * NCH + i)

            if q == 1:

                @pl.when(x == 3)
                def _():
                    to_cross(src, five, i, 2 * NCH + i)

            @pl.when(p == 0)
            def _():
                to_sibling(src, 1, q, i)

            @pl.when(p == 1)
            def _():
                to_sibling(src, 0, q, i)

    def on_minus_of(q, i, here):
        @pl.when(jnp.logical_and(holder, here))
        def _():
            src = rows(rights[2][q], i)
            landed(src, rminus.at[q * NCH + i])
            if q == 1:

                @pl.when(x != 0)
                def _():
                    to_minus(src, rights[3][1], i, 2 * NCH + i)

            if q == 0:

                @pl.when(x == 0)
                def _():
                    to_cross(src, five, i, 2 * NCH + i)

            to_sibling(src, 2, q, i)

    def on_plus(late, i):
        on_plus_of(late, i, x != 0)
        on_plus_of(1 - late, i, x == 0)

    def on_minus(late, i):
        on_minus_of(1 - late, i, x != 3)
        on_minus_of(late, i, x == 3)

    def on_five(i):
        @pl.when(jnp.logical_and(holder, x == 3))
        def _():
            landed(rows(five, i), rcross.at[2 * NCH + i])
            to_plus(rows(five, i), rights[3][0], i, 2 * NCH + i)

        @pl.when(jnp.logical_and(holder, x == 0))
        def _():
            landed(rows(five, i), rcross.at[2 * NCH + i])
            to_minus(rows(five, i), rights[3][1], i, 2 * NCH + i)

    def on_last(i):
        @pl.when(holder)
        def _():
            src = rows(rights[3][1], i)
            landed(src, rminus.at[2 * NCH + i])
            to_sibling(src, 3, 1, i)
            src = rows(rights[3][0], i)
            landed(src, rplus.at[2 * NCH + i])
            to_sibling(src, 3, 0, i)

    def left_ready(n):
        landed(five_of(lefts[n], rep), l_left.at[n])

        @pl.when(holder)
        def _():
            landed(five_of(lefts[n], mate), l_part.at[n])

    def right_ready(n, q):
        if n == 0 and q == 0:

            @pl.when(holder)
            def _():
                landed(rights[0][0], l_own)

        @pl.when(jnp.logical_not(holder))
        def _():
            landed(rights[n][q], rd.at[2 * n + q])

    def multiply(n, q):
        total = out_ref if q == 0 else partial

        def slot(j, acc):
            a = lefts[n][meta_sm[q, n, 0, j]]
            b = rights[n][q][meta_sm[q, n, 1, j]]
            a_hi = a.astype(jnp.bfloat16)
            a_lo = (a - a_hi.astype(jnp.float32)).astype(jnp.bfloat16)
            b_hi = b.astype(jnp.bfloat16)
            b_lo = (b - b_hi.astype(jnp.float32)).astype(jnp.bfloat16)
            prod = jnp.dot(
                jnp.concatenate([a_hi, a_lo], axis=1),
                jnp.concatenate([b_hi, b_hi], axis=0),
                preferred_element_type=jnp.float32,
            ) + jnp.dot(a_hi, b_lo, preferred_element_type=jnp.float32)
            acc = prod + jnp.where(meta_sm[q, n, 2, j] > 0, acc, 0.0)
            sums[j] = acc
            return acc

        lax.fori_loop(0, NTASK, slot, jnp.zeros((TILE, TILE), jnp.float32))

        def collect(c, carry):
            got = jnp.where(meta_sm[q, n, 4, c] > 0, sums[meta_sm[q, n, 3, c]], 0.0)
            if n == 0:
                total[c] = got
            else:
                total[c] += got
            return carry

        lax.fori_loop(0, NC, collect, 0)

    start()
    for i in range(NCH):
        on_cross(1, i)
        on_plus(0, i)
        on_minus(0, i)
        on_mate(i)
        if i == 0:
            on_z(0, 0)
            on_z(0, 1)
        if i == 1:
            send_own_left(2)
            on_z(1, 0)
        if i == 2:
            send_own_left(3)
            on_z(2, 0)
        if i == 3:
            on_z(1, 1)
    on_meta()
    left_ready(0)
    right_ready(0, 0)
    multiply(0, 0)
    on_z(2, 1)
    on_cross(0, 0)
    right_ready(0, 1)
    multiply(0, 1)
    for i in range(NCH):
        if i > 0:
            on_cross(0, i)
        on_plus(1, i)
        on_minus(1, i)
        if i == 0:
            on_z(0, 2)
        if i == 1:
            on_z(1, 2)
        if i == 2:
            on_z(0, 3)
        if i == 3:
            on_z(1, 3)
    left_ready(1)
    for q in range(2):
        right_ready(1, q)
        multiply(1, q)
        on_five(2 * q)
        on_five(2 * q + 1)
    on_z(2, 2)
    left_ready(2)
    for q in range(2):
        right_ready(2, q)
        multiply(2, q)
        on_last(2 * q)
        on_last(2 * q + 1)
    on_z(2, 3)
    left_ready(3)
    right_ready(3, 1)
    multiply(3, 1)
    for g in range(4):
        part = pl.ds(4 * g, 4)
        remote(partial.at[part], arrived.at[part], sc.at[g], rc.at[g], at_mate).start()
    right_ready(3, 0)
    multiply(3, 0)
    for g in range(4):
        part = pl.ds(4 * g, 4)
        landed(arrived.at[part], rc.at[g])
        out_ref[part] += arrived[part]

    for n in range(4):
        landed(meta_in.at[n], smeta.at[n])
        landed(partial.at[pl.ds(4 * n, 4)], sc.at[n])
        for kind in range(3):
            for side in range(2):
                landed(five_of(lefts[n], 0), sz.at[side, kind, n])

    @pl.when(holder)
    def _():
        for i in range(NCH):
            landed(five_of(lefts[0], 0), sy.at[i])
        for slot in range(3 * NCH):
            landed(rows(five, 0), splus.at[slot])
            landed(rows(five, 0), sminus.at[slot])
        for slot in range(2 * NCH):
            landed(rows(five, 0), scross.at[slot])

        @pl.when(jnp.logical_or(x == 0, x == 3))
        def _():
            for i in range(NCH):
                landed(rows(five, 0), scross.at[2 * NCH + i])

        for b in range(8):
            landed(five, sd.at[b])

    @pl.when(jnp.logical_not(holder))
    def _():
        for i in range(NCH):
            landed(rows(five, 0), sy.at[i])


def gather_and_multiply(p_tiles, meta):
    dma = pltpu.SemaphoreType.DMA
    block = pltpu.VMEM((NT, TILE, TILE), jnp.float32)
    target = pltpu.VMEM((NC, TILE, TILE), jnp.float32)
    return pl.pallas_call(
        kernel,
        out_shape=jax.ShapeDtypeStruct((NC, TILE, TILE), jnp.float32),
        in_specs=[pl.BlockSpec(memory_space=pl.ANY)] * 2,
        out_specs=pl.BlockSpec(memory_space=pltpu.VMEM),
        scratch_shapes=[block] * 15
        + [
            pltpu.VMEM((NTASK, TILE, TILE), jnp.float32),
            target,
            target,
            pltpu.VMEM((4, 8, 128), jnp.int32),
            pltpu.SMEM((2, 4, 8, 128), jnp.int32),
        ]
        + [dma((4,)), dma((12,)), dma((12,)), dma((12,)), dma((2, 3, 4)), dma((8,)), dma((4,)), dma((4,))] * 2
        + [dma, dma((4,)), dma((4,)), dma((2, 4))],
        compiler_params=pltpu.CompilerParams(
            collective_id=0, has_side_effects=True, vmem_limit_bytes=60 * 1024 * 1024
        ),
    )(p_tiles, meta)


def per_device(p_tiles, tasks):
    own = p_tiles.reshape(NT, TILE, TILE)
    return gather_and_multiply(own, sort_tasks(tasks[0, 0]))[None, None]


def solution(mesh):
    return jax.shard_map(
        per_device,
        mesh=mesh,
        in_specs=(P("blk", "rep", None, None, None, None), P("blk", "rep", None, None, None)),
        out_specs=P("blk", "rep", None, None, None),
        check_vma=False,
    )
```

```python
import jax
import jax.numpy as jnp
from jax import lax
from jax.experimental import pallas as pl
from jax.experimental.pallas import tpu as pltpu
from jax.sharding import PartitionSpec as P

MESH = pl.DeviceIdType.MESH
TILE = 128
NT = 40
TPS = 5
NC = 16
NTASK = 48
CH = 10
NCH = NT // CH
ORDER_OF_CHUNK = (0, 1, 3, 2)


def sort_tasks(tasks):
    left, right, target = tasks[:, 0], tasks[:, 1], tasks[:, 2]
    slots = jnp.arange(NTASK, dtype=jnp.int32)
    before = (target[:, None, :] < target[:, :, None]) | (
        (target[:, None, :] == target[:, :, None]) & (slots[None, None, :] < slots[None, :, None])
    )
    rank = jnp.sum(before.astype(jnp.int32), axis=2)
    place = (rank[:, :, None] == slots[None, None, :]).astype(jnp.int32)
    pick = lambda v: jnp.sum(place * v[:, :, None], axis=1)
    sorted_target = pick(target)
    same = jnp.concatenate(
        [jnp.zeros_like(target[:, :1]), (sorted_target[:, 1:] == sorted_target[:, :-1]).astype(jnp.int32)], axis=1
    )
    cols = jnp.arange(NC, dtype=jnp.int32)
    count = jnp.sum((target[:, :, None] == cols).astype(jnp.int32), axis=1)
    upto = jnp.sum((target[:, :, None] <= cols).astype(jnp.int32), axis=1)
    last = jnp.maximum(upto - 1, 0)
    wide = lambda v: jnp.pad(v, ((0, 0), (0, 128 - v.shape[1])))
    rows = [wide(jnp.clip(pick(left), 0, NT - 1)), wide(jnp.clip(pick(right), 0, NT - 1)), wide(same), wide(last)]
    rows.append(wide((count > 0).astype(jnp.int32)))
    rows += [jnp.zeros_like(rows[0])] * 3
    return jnp.stack(rows, axis=1)


def kernel(p_ref, meta_ref, out_ref, *scratch):
    lefts = scratch[0:4]
    rights = (scratch[4:6], scratch[6:8], scratch[8:10], scratch[10:12])
    four = scratch[12:14]
    (five, sums, partial, arrived, meta_in, meta_sm) = scratch[14:20]
    (ry, rplus, rminus, rcross, rz, rd, rmeta, rc) = scratch[20:28]
    (sy, splus, sminus, scross, sz, sd, smeta, sc) = scratch[28:36]
    (l_own, l_left, l_part, l_meta) = scratch[36:40]

    blk, rep = lax.axis_index("blk"), lax.axis_index("rep")
    h, x, k = blk // 8, (blk % 8) // 2, blk % 2
    z, lo = rep // 2, rep % 2
    p = (lo + h) % 2
    holder = k == p
    mate = rep + 1 - 2 * lo
    at_plus = (h * 8 + ((x + 1) % 4) * 2 + k, rep)
    at_minus = (h * 8 + ((x + 3) % 4) * 2 + k, rep)
    at_mate = (blk, mate)
    at_cross = ((1 - h) * 8 + x * 2 + k, mate)
    at_zp = (blk, ((z + 1) % 4) * 2 + lo)
    at_zm = (blk, ((z + 3) % 4) * 2 + lo)
    at_sib = (blk + 1 - 2 * k, rep)

    def s_of(n, parity):
        odd = (k + parity) % 2
        f = (1 - k) * parity
        return odd + (0, 2, 6, 4)[n] + f * (0, 4, -2, -2)[n]

    barrier = pltpu.get_barrier_semaphore()
    for peer in (at_plus, at_minus, at_mate, at_cross, at_zp, at_zm, at_sib):
        pl.semaphore_signal(barrier, inc=1, device_id=peer, device_id_type=MESH)
    pl.semaphore_wait(barrier, 7)

    def remote(src, dst, ssem, rsem, peer):
        return pltpu.make_async_remote_copy(
            src_ref=src, dst_ref=dst, send_sem=ssem, recv_sem=rsem, device_id=peer, device_id_type=MESH
        )

    def rows(ref, i):
        return ref.at[pl.ds(CH * i, CH)]

    def five_of(ref, r):
        return ref.at[pl.ds(TPS * r, TPS)]

    def landed(ref, sem):
        pltpu.make_async_copy(ref, ref, sem).wait()

    def to_plus(src, dst, i, slot):
        remote(src, rows(dst, i), splus.at[slot], rplus.at[slot], at_plus).start()

    def to_minus(src, dst, i, slot):
        remote(src, rows(dst, i), sminus.at[slot], rminus.at[slot], at_minus).start()

    def to_cross(src, dst, i, slot):
        remote(src, rows(dst, i), scross.at[slot], rcross.at[slot], at_cross).start()

    def to_sibling(src, n, q, i):
        remote(src, rows(rights[n][q], i), sd.at[2 * n + q], rd.at[2 * n + q], at_sib).start()

    def z_both(src, n, r, kind):
        dst = five_of(lefts[n], r)
        remote(src, dst, sz.at[0, kind, n], rz.at[0, kind, n], at_zp).start()
        remote(src, dst, sz.at[1, kind, n], rz.at[1, kind, n], at_zm).start()

    def own_left(n):
        return p_ref.at[pl.ds(TPS * s_of(n, p), TPS)]

    def left_to_mate(n):
        @pl.when(holder)
        def _():
            src = p_ref.at[pl.ds(TPS * s_of(n, 1 - p), TPS)]
            remote(src, five_of(lefts[n], rep), sy.at[n], ry.at[n], at_mate).start()

    def own_to_minus(i):
        @pl.when(jnp.logical_and(holder, x == 0))
        def _():
            to_minus(rows(p_ref, i), rights[2][0], i, i)

    def start():
        @pl.when(jnp.logical_not(holder))
        def _():
            for i in range(NCH):
                remote(rows(p_ref, i), rows(rights[0][1], i), sy.at[i], ry.at[i], at_mate).start()

        for n in range(2):
            send_own_left(n)
        left_to_mate(0)

        @pl.when(holder)
        def _():
            for i in range(NCH):
                src = rows(p_ref, i)

                @pl.when(x != 3)
                def _():
                    to_plus(src, rights[1][0], i, i)

                to_cross(src, four[1], i, NCH + i)

            own_to_minus(0)
            own_to_minus(1)

            @pl.when(p == 0)
            def _():
                remote(p_ref, rights[0][0], sd.at[0], rd.at[0], at_sib).start()

            pltpu.make_async_copy(p_ref, rights[0][0], l_own).start()

        for n in range(4):
            pltpu.make_async_copy(own_left(n), five_of(lefts[n], rep), l_left.at[n]).start()
            remote(meta_ref.at[s_of(n, 1 - p)], meta_in.at[n], smeta.at[n], rmeta.at[n], at_mate).start()
            pltpu.make_async_copy(meta_ref.at[s_of(n, p)], meta_sm.at[0, n], l_meta.at[0, n]).start()

    def on_meta():
        for n in range(4):
            landed(meta_in.at[n], rmeta.at[n])
            pltpu.make_async_copy(meta_in.at[n], meta_sm.at[1, n], l_meta.at[1, n]).start()
        for q in range(2):
            for n in range(4):
                landed(meta_sm.at[q, n], l_meta.at[q, n])

    def on_mate(i):
        @pl.when(holder)
        def _():
            n = ORDER_OF_CHUNK[i]
            src = rows(rights[0][1], i)
            landed(src, ry.at[i])
            head = rights[0][1].at[pl.ds(CH * i, TPS)]
            pltpu.make_async_copy(head, five_of(lefts[n], mate), l_part.at[n]).start()

            @pl.when(x != 3)
            def _():
                to_plus(src, rights[1][1], i, NCH + i)

            @pl.when(x == 0)
            def _():
                to_minus(src, rights[2][1], i, NCH + i)

            to_cross(src, four[0], i, i)

            @pl.when(p == 0)
            def _():
                to_sibling(src, 0, 1, i)

        @pl.when(jnp.logical_not(holder))
        def _():
            landed(five_of(lefts[i], mate), ry.at[i])

    def send_mate_left(n):
        @pl.when(holder)
        def _():
            z_both(rights[0][1].at[pl.ds(CH * ORDER_OF_CHUNK[n], TPS)], n, mate, 1)

        @pl.when(jnp.logical_not(holder))
        def _():
            z_both(five_of(lefts[n], mate), n, mate, 1)

    def send_own_left(n):
        z_both(own_left(n), n, rep, 0)

    def on_z(kind, n):
        for side in range(2):
            away = (z + 3) % 4 if side == 0 else (z + 1) % 4
            if kind == 2:
                away = (z + 2) % 4
            own_side = kind == 0 or (kind == 2 and side == 0)
            r = away * 2 + (lo if own_side else 1 - lo)
            src = five_of(lefts[n], r)
            landed(src, rz.at[side, kind, n])
            if kind == 0 and side == 0:
                remote(src, src, sz.at[0, 2, n], rz.at[0, 2, n], at_zp).start()
            if kind == 1 and side == 1:
                remote(src, src, sz.at[1, 2, n], rz.at[1, 2, n], at_zm).start()

    def on_cross(q, i):
        @pl.when(holder)
        def _():
            src = rows(four[q], i)
            landed(src, rcross.at[q * NCH + i])

            @pl.when(x == 3)
            def _():
                to_plus(src, rights[1][q], i, q * NCH + i)

            @pl.when(x != 0)
            def _():
                to_minus(src, rights[2][q], i, q * NCH + i)

            @pl.when(p == 1)
            def _():
                to_sibling(src, 1, q, i)

    def on_plus_of(q, i, here):
        @pl.when(jnp.logical_and(holder, here))
        def _():
            src = rows(rights[1][q], i)
            landed(src, rplus.at[q * NCH + i])
            if q == 0:

                @pl.when(x == 0)
                def _():
                    to_plus(src, rights[3][0], i, 2 * NCH + i)

            if q == 1:

                @pl.when(x == 2)
                def _():
                    to_plus(src, rights[3][1], i, 2 * NCH + i)

                @pl.when(x == 3)
                def _():
                    to_cross(src, five, i, 2 * NCH + i)

            @pl.when(p == 0)
            def _():
                to_sibling(src, 1, q, i)

            @pl.when(p == 1)
            def _():
                to_sibling(src, 0, q, i)

    def second_to_plus(i):
        @pl.when(jnp.logical_and(holder, x == 1))
        def _():
            to_plus(rows(rights[1][0], i), rights[3][0], i, 2 * NCH + i)

    def on_minus_of(q, i, here):
        @pl.when(jnp.logical_and(holder, here))
        def _():
            src = rows(rights[2][q], i)
            landed(src, rminus.at[q * NCH + i])
            if q == 1:

                @pl.when(x != 0)
                def _():
                    to_minus(src, rights[3][1], i, 2 * NCH + i)

                @pl.when(x == 0)
                def _():
                    to_cross(src, five, i, 2 * NCH + i)

            to_sibling(src, 2, q, i)

    def on_plus(late, i):
        on_plus_of(late, i, x != 0)
        on_plus_of(1 - late, i, x == 0)

    def on_five(i):
        @pl.when(jnp.logical_and(holder, x == 3))
        def _():
            landed(rows(five, i), rcross.at[2 * NCH + i])
            to_plus(rows(five, i), rights[3][0], i, 2 * NCH + i)

        @pl.when(jnp.logical_and(holder, x == 0))
        def _():
            landed(rows(five, i), rcross.at[2 * NCH + i])
            to_minus(rows(five, i), rights[3][0], i, 2 * NCH + i)

    def on_last(q, i):
        for here, sem in ((x == 3, (rminus, rplus)[q]), (x != 3, (rplus, rminus)[q])):

            @pl.when(jnp.logical_and(holder, here))
            def _():
                src = rows(rights[3][q], i)
                landed(src, sem.at[2 * NCH + i])
                to_sibling(src, 3, q, i)

    def left_ready(n):
        landed(five_of(lefts[n], rep), l_left.at[n])

        @pl.when(holder)
        def _():
            landed(five_of(lefts[n], mate), l_part.at[n])

    def right_ready(n, q):
        if n == 0 and q == 0:

            @pl.when(holder)
            def _():
                landed(rights[0][0], l_own)

        @pl.when(jnp.logical_not(holder))
        def _():
            landed(rights[n][q], rd.at[2 * n + q])

    def multiply(n, q):
        total = out_ref if q == 0 else partial

        def slot(j, acc):
            a = lefts[n][meta_sm[q, n, 0, j]]
            b = rights[n][q][meta_sm[q, n, 1, j]]
            a_hi = a.astype(jnp.bfloat16)
            a_lo = (a - a_hi.astype(jnp.float32)).astype(jnp.bfloat16)
            b_hi = b.astype(jnp.bfloat16)
            b_lo = (b - b_hi.astype(jnp.float32)).astype(jnp.bfloat16)
            both = jnp.dot(
                jnp.concatenate([a_hi, a_lo], axis=1),
                jnp.concatenate(
                    [jnp.concatenate([b_hi, b_hi], axis=0), jnp.concatenate([b_lo, jnp.zeros_like(b_lo)], axis=0)], axis=1
                ),
                preferred_element_type=jnp.float32,
            )
            prod = both[:, :TILE] + both[:, TILE:]
            acc = prod + jnp.where(meta_sm[q, n, 2, j] > 0, acc, 0.0)
            sums[j] = acc
            return acc

        lax.fori_loop(0, NTASK, slot, jnp.zeros((TILE, TILE), jnp.float32), unroll=8)

        def collect(c, carry):
            got = jnp.where(meta_sm[q, n, 4, c] > 0, sums[meta_sm[q, n, 3, c]], 0.0)
            if n == 0:
                total[c] = got
            else:
                total[c] += got
            return carry

        lax.fori_loop(0, NC, collect, 0)

    def products(n, q):
        right_ready(n, q)
        multiply(n, q)

    start()
    on_cross(1, 0)
    on_z(0, 0)
    on_mate(0)
    send_mate_left(0)
    on_plus(0, 0)
    on_minus_of(1, 0, x != 3)
    on_z(0, 1)
    left_to_mate(1)
    on_cross(1, 1)
    on_mate(1)
    send_own_left(2)
    on_plus(0, 1)
    on_minus_of(1, 1, x != 3)
    on_cross(1, 2)
    left_to_mate(2)
    on_minus_of(1, 0, x == 3)
    on_mate(2)
    on_z(1, 0)
    send_mate_left(1)
    on_plus(0, 2)
    on_minus_of(1, 2, x != 3)
    on_cross(1, 3)
    left_to_mate(3)
    on_minus_of(1, 1, x == 3)
    on_mate(3)
    own_to_minus(2)
    own_to_minus(3)
    send_own_left(3)
    on_plus(0, 3)
    on_minus_of(1, 3, x != 3)
    for i in range(NCH):
        second_to_plus(i)
    on_minus_of(1, 2, x == 3)
    on_z(2, 0)
    on_cross(0, 0)
    on_plus(1, 0)
    on_z(0, 2)
    send_mate_left(2)
    on_minus_of(1, 3, x == 3)
    on_cross(0, 1)
    on_plus(1, 1)
    on_z(1, 1)
    send_mate_left(3)
    on_meta()
    on_cross(0, 2)
    on_plus(1, 2)
    on_z(0, 3)
    left_ready(0)
    products(0, 1)
    on_z(2, 1)
    on_cross(0, 3)
    on_plus(1, 3)
    on_z(1, 2)
    on_five(0)
    left_ready(1)
    products(1, 1)
    on_z(1, 3)
    on_five(1)
    products(0, 0)
    on_five(2)
    products(1, 0)
    on_z(2, 2)
    on_five(3)
    left_ready(2)
    products(2, 1)
    for i in range(NCH):
        on_last(1, i)
    on_z(2, 3)
    left_ready(3)
    products(3, 1)
    for i in range(NCH):
        on_minus_of(0, i, x >= 0)
    for g in range(4):
        part = pl.ds(4 * g, 4)
        remote(partial.at[part], arrived.at[part], sc.at[g], rc.at[g], at_mate).start()
    products(2, 0)
    for i in range(NCH):
        on_last(0, i)
    products(3, 0)
    for g in range(4):
        part = pl.ds(4 * g, 4)
        landed(arrived.at[part], rc.at[g])
        out_ref[part] += arrived[part]

    for n in range(4):
        landed(meta_in.at[n], smeta.at[n])
        landed(partial.at[pl.ds(4 * n, 4)], sc.at[n])
        for kind in range(3):
            for side in range(2):
                landed(five_of(lefts[n], 0), sz.at[side, kind, n])

    @pl.when(holder)
    def _():
        for i in range(NCH):
            landed(five_of(lefts[0], 0), sy.at[i])
        for slot in range(3 * NCH):
            landed(rows(five, 0), splus.at[slot])
            landed(rows(five, 0), sminus.at[slot])
        for slot in range(2 * NCH):
            landed(rows(five, 0), scross.at[slot])

        @pl.when(jnp.logical_or(x == 0, x == 3))
        def _():
            for i in range(NCH):
                landed(rows(five, 0), scross.at[2 * NCH + i])

        for b in range(8):
            landed(five, sd.at[b])

    @pl.when(jnp.logical_not(holder))
    def _():
        for i in range(NCH):
            landed(rows(five, 0), sy.at[i])


def gather_and_multiply(p_tiles, meta):
    dma = pltpu.SemaphoreType.DMA
    block = pltpu.VMEM((NT, TILE, TILE), jnp.float32)
    target = pltpu.VMEM((NC, TILE, TILE), jnp.float32)
    return pl.pallas_call(
        kernel,
        out_shape=jax.ShapeDtypeStruct((NC, TILE, TILE), jnp.float32),
        in_specs=[pl.BlockSpec(memory_space=pl.ANY)] * 2,
        out_specs=pl.BlockSpec(memory_space=pltpu.VMEM),
        scratch_shapes=[block] * 15
        + [
            pltpu.VMEM((NTASK, TILE, TILE), jnp.float32),
            target,
            target,
            pltpu.VMEM((4, 8, 128), jnp.int32),
            pltpu.SMEM((2, 4, 8, 128), jnp.int32),
        ]
        + [dma((4,)), dma((12,)), dma((12,)), dma((12,)), dma((2, 3, 4)), dma((8,)), dma((4,)), dma((4,))] * 2
        + [dma, dma((4,)), dma((4,)), dma((2, 4))],
        compiler_params=pltpu.CompilerParams(
            collective_id=0, has_side_effects=True, vmem_limit_bytes=60 * 1024 * 1024
        ),
    )(p_tiles, meta)


def per_device(p_tiles, tasks):
    own = p_tiles.reshape(NT, TILE, TILE)
    return gather_and_multiply(own, sort_tasks(tasks[0, 0]))[None, None]


def solution(mesh):
    return jax.shard_map(
        per_device,
        mesh=mesh,
        in_specs=(P("blk", "rep", None, None, None, None), P("blk", "rep", None, None, None)),
        out_specs=P("blk", "rep", None, None, None),
        check_vma=False,
    )
```

```python
import jax
import jax.numpy as jnp
from jax import lax
from jax.experimental import pallas as pl
from jax.experimental.pallas import tpu as pltpu
from jax.sharding import PartitionSpec as P

MESH = pl.DeviceIdType.MESH
TILE = 128
NT = 40
TPS = 5
NC = 16
NTASK = 48
CH = 10
NCH = NT // CH
ORDER_OF_CHUNK = (0, 1, 3, 2)

SCHEDULE = (
    (
        ("C4", "P0", "M0", "C5", "P1", "M1", "Z000", "Z100", "Z001", "Z101", "Z002", "Z102", "Z003", "Z103", "C6",
         "z100", "z000", "Z020", "y0", "c4", "z101", "z001", "P4", "M4", "Z010", "Z110", "Z021", "C7", "z102", "z002",
         "Z022", "y1", "c5", "z103", "z003", "P5", "M5", "Z111", "m4", "p4", "C8", "z110", "z020", "Z120", "Z011",
         "z010", "z111", "y2", "c6", "Z121", "P6", "M6", "Z113", "G", "p5", "m5", "C9", "z120", "z021", "Y0", "Y1",
         "Y2", "Z023", "Y3", "y3", "c7", "P7", "M7", "Z112", "z121", "z022", "m8", "p6", "P2", "M2", "Z013", "c8"),
        ("z113", "z011", "Z123", "m6", "p7", "C10", "P3", "M3", "Z012", "c9", "z112", "z023", "Z122", "m7", "p0",
         "C11", "C0", "P8", "M8"),
        ("c10", "z123", "z013", "m9", "p1", "C1", "P9", "M9"),
        ("c11", "z122", "z012", "m10", "p2", "C2", "P10", "M10", "c0"),
        ("m11", "p3", "C3", "P11", "M11", "c1"),
        (),
        ("m0", "p8", "c2", "m1", "p9", "c3"),
        ("m2", "p10", "m3", "p11"),
        (),
        (),
    ),
    (
        ("C4", "P0", "C5", "P1", "Z000", "Z100", "Z001", "Z101", "Z002", "Z102", "Z003", "Z103", "C6", "z100", "z000",
         "Z020", "p0", "y0", "c4", "z101", "z001", "P4", "Z010", "Z110", "M4", "Z021", "C7", "z102", "z002", "Z022",
         "y1", "p1", "c5", "z103", "z003", "P5", "Z111", "M5", "m4", "M8", "C0", "z110", "z020", "Z120", "Z011",
         "z010", "z111", "y2", "p4", "c6", "Z121", "P6", "Z113", "M6", "G", "m5", "C1", "z120", "z021", "Y0", "Y1",
         "Y2", "Z023", "Y3", "y3", "p5", "c7", "P7", "Z112", "M7", "z121", "z022", "m8", "P2", "C2", "Z013", "M9",
         "p6", "c0"),
        ("z113", "z011", "Z123", "m6", "P3", "C3", "Z012", "M10", "p7", "c1", "z112", "z023", "Z122", "m7", "P8"),
        ("M11", "c2", "p2", "z123", "z013", "m9", "P9"),
        ("M0", "c3", "p3", "z122", "z012", "m10", "P10", "M1", "p8"),
        ("m11", "P11", "M2", "p9"),
        (),
        ("m0", "M3", "p10", "m1", "p11"),
        ("m2", "m3"),
        (),
        (),
    ),
    (
        ("C4", "P0", "C5", "P1", "Z000", "Z100", "Z001", "Z101", "Z002", "Z102", "Z003", "Z103", "C6", "z100", "z000",
         "Z020", "p0", "y0", "c4", "z101", "z001", "P4", "Z010", "Z110", "M4", "Z021", "C7", "z102", "z002", "Z022",
         "y1", "p1", "c5", "z103", "z003", "P5", "Z111", "M5", "m4", "M8", "C0", "z110", "z020", "Z120", "Z011",
         "z010", "z111", "y2", "c6", "p4", "Z121", "P6", "Z113", "M6", "G", "m5", "C1", "z120", "z021", "Y0", "Y1",
         "Y2", "Z023", "Y3", "y3", "p5", "c7", "P7", "Z112", "M7", "z121", "z022", "m6", "P8", "C2", "Z013", "M9",
         "p6", "c0"),
        ("z113", "z011", "Z123", "m7", "P9", "C3", "Z012", "M10", "p7", "c1", "z112", "z023", "Z122", "m8", "P10"),
        ("M11", "p2", "c2", "z123", "z013", "m9", "P11"),
        ("M0", "c3", "p3", "z122", "z012", "m10", "P2", "M1", "p8"),
        ("m11", "P3", "M2", "p9"),
        (),
        ("m0", "M3", "p10", "m1", "p11"),
        ("m2", "m3"),
        (),
        (),
    ),
    (
        ("C4", "C5", "Z000", "Z100", "Z001", "Z101", "Z002", "Z102", "Z003", "Z103", "C6", "z100", "z000", "Z020",
         "m0", "p0", "y0", "c4", "z101", "z001", "Z010", "Z110", "P4", "M4", "Z021", "C7", "z102", "z002", "Z022",
         "y1", "m1", "p1", "c5", "z103", "z003", "Z111", "P5", "M5", "C0", "z110", "z020", "Z120", "Z011", "z010",
         "z111", "y2", "m4", "p4", "c6", "Z121", "Z113", "P6", "M6", "G", "C1", "z120", "z021", "Y0", "Y1", "Y2",
         "Z023", "M8", "Y3", "y3", "m5", "c7", "p5", "Z112", "P7", "M7", "z121", "z022", "C2", "Z013", "M9", "m6",
         "p6", "c0", "P0"),
        ("z113", "z011", "Z123", "C3", "Z012", "M10", "p7", "m7", "c1", "P1", "z112", "z023", "Z122", "C8"),
        ("M11", "p8", "c2", "m2", "P2", "z123", "z013", "C9"),
        ("M0", "p9", "c3", "m3", "P3", "z122", "z012", "C10", "M1", "p10", "c8", "m8", "P8"),
        ("C11", "M2", "p11", "c9", "m9", "P9"),
        (),
        ("M3", "p2", "c10", "m10", "P10", "p3", "c11", "m11", "P11"),
        (),
        (),
        (),
    ),
    (
        ("B0", "B1", "B2", "B3", "Z000", "Z100", "Z001", "Z101", "Z002", "Z102", "y0", "z100", "z000", "y1", "Z003",
         "Z103", "y2", "z101", "z001", "y3", "Z010", "Z110", "z102", "z002", "Z111", "Z020", "Z011", "Z112", "z103",
         "z003", "Z012", "Z113", "Z021", "z110", "z010", "Z120", "Z013", "z020", "z111", "Z121", "Z022", "z011",
         "z112", "Z122", "Z023", "z012", "z113", "Z123", "z021", "z120"),
        ("z013", "z121"),
        ("z022", "z122"),
        ("z023", "z123"),
        (),
        (),
        (),
        (),
        (),
        (),
    ),
)
HOLDER_TURNS = ((0, 1), (0, 0), (1, 1), (2, 1), (3, 1), None, (1, 0), (2, 0), (3, 0))
SIBLING_TURNS = ((0, 1), (1, 1), (2, 1), (3, 1), None, (0, 0), (1, 0), (2, 0), (3, 0))


FIRST_OF_SIBLING = next(op for segment in SCHEDULE[4] for op in segment if op[0] == "Z")


def sort_tasks(tasks):
    left, right, target = tasks[:, 0], tasks[:, 1], tasks[:, 2]
    slots = jnp.arange(NTASK, dtype=jnp.int32)
    before = (target[:, None, :] < target[:, :, None]) | (
        (target[:, None, :] == target[:, :, None]) & (slots[None, None, :] < slots[None, :, None])
    )
    rank = jnp.sum(before.astype(jnp.int32), axis=2)
    place = (rank[:, :, None] == slots[None, None, :]).astype(jnp.int32)
    pick = lambda v: jnp.sum(place * v[:, :, None], axis=1)
    sorted_target = pick(target)
    same = jnp.concatenate(
        [jnp.zeros_like(target[:, :1]), (sorted_target[:, 1:] == sorted_target[:, :-1]).astype(jnp.int32)], axis=1
    )
    cols = jnp.arange(NC, dtype=jnp.int32)
    count = jnp.sum((target[:, :, None] == cols).astype(jnp.int32), axis=1)
    upto = jnp.sum((target[:, :, None] <= cols).astype(jnp.int32), axis=1)
    last = jnp.maximum(upto - 1, 0)
    wide = lambda v: jnp.pad(v, ((0, 0), (0, 128 - v.shape[1])))
    rows = [wide(jnp.clip(pick(left), 0, NT - 1)), wide(jnp.clip(pick(right), 0, NT - 1)), wide(same), wide(last)]
    rows.append(wide((count > 0).astype(jnp.int32)))
    rows += [jnp.zeros_like(rows[0])] * 3
    return jnp.stack(rows, axis=1)


def kernel(p_ref, meta_ref, out_ref, *scratch):
    lefts = scratch[0:4]
    rights = (scratch[4:6], scratch[6:8], scratch[8:10], scratch[10:12])
    four = scratch[12:14]
    (five, sums, partial, arrived, meta_in, meta_sm) = scratch[14:20]
    (ry, rplus, rminus, rcross, rz, rd, rmeta, rc) = scratch[20:28]
    (sy, splus, sminus, scross, sz, sd, smeta, sc) = scratch[28:36]
    (l_own, l_left, l_part, l_meta, go) = scratch[36:41]

    blk, rep = lax.axis_index("blk"), lax.axis_index("rep")
    h, x, k = blk // 8, (blk % 8) // 2, blk % 2
    z, lo = rep // 2, rep % 2
    p = (lo + h) % 2
    holder = k == p
    mate = rep + 1 - 2 * lo
    at_plus = (h * 8 + ((x + 1) % 4) * 2 + k, rep)
    at_minus = (h * 8 + ((x + 3) % 4) * 2 + k, rep)
    at_mate = (blk, mate)
    at_cross = ((1 - h) * 8 + x * 2 + k, mate)
    at_zp = (blk, ((z + 1) % 4) * 2 + lo)
    at_zm = (blk, ((z + 3) % 4) * 2 + lo)
    at_sib = (blk + 1 - 2 * k, rep)

    def s_of(n, parity):
        odd = (k + parity) % 2
        f = (1 - k) * parity
        return odd + (0, 2, 6, 4)[n] + f * (0, 4, -2, -2)[n]

    barrier = pltpu.get_barrier_semaphore()
    for peer in (at_plus, at_minus, at_mate, at_cross, at_zp, at_zm, at_sib):
        pl.semaphore_signal(barrier, inc=1, device_id=peer, device_id_type=MESH)
    pl.semaphore_wait(barrier, 7)

    def remote(src, dst, ssem, rsem, peer):
        return pltpu.make_async_remote_copy(
            src_ref=src, dst_ref=dst, send_sem=ssem, recv_sem=rsem, device_id=peer, device_id_type=MESH
        )

    def rows(ref, i):
        return ref.at[pl.ds(CH * i, CH)]

    def five_of(ref, r):
        return ref.at[pl.ds(TPS * r, TPS)]

    def landed(ref, sem):
        pltpu.make_async_copy(ref, ref, sem).wait()

    def own(q, i):
        return rows(p_ref, i) if q == 0 else rows(rights[0][1], i)

    def to_sibling(here, src, n, q, i):
        @pl.when(here)
        def _():
            remote(src, rows(rights[n][q], i), sd.at[2 * n + q], rd.at[2 * n + q], at_sib).start()

    def sliver_of(side, kind):
        away = (z + 2) % 4 if kind == 2 else (z + 3) % 4 if side == 0 else (z + 1) % 4
        return away * 2 + (lo if kind == 0 or (kind == 2 and side == 0) else 1 - lo)

    def wait_z(side, kind, n):
        landed(five_of(lefts[n], sliver_of(side, kind)), rz.at[side, kind, n])

    def send_z(side, kind, n, held):
        if kind == 0:
            src, r = p_ref.at[pl.ds(TPS * s_of(n, p), TPS)], rep
        elif kind == 1:
            r = mate
            src = rights[0][1].at[pl.ds(CH * ORDER_OF_CHUNK[n], TPS)] if held else five_of(lefts[n], r)
        else:
            r = sliver_of(side, side)
            src = five_of(lefts[n], r)
        peer = (at_zp, at_zm)[side]
        remote(src, five_of(lefts[n], r), sz.at[side, kind, n], rz.at[side, kind, n], peer).start()

    def holder_op(op, x):
        what = op[0]
        if what == "G":
            pl.semaphore_signal(go, inc=1, device_id=at_sib, device_id_type=MESH)
            return
        if what == "z":
            wait_z(int(op[1]), int(op[2]), int(op[3]))
            return
        if what == "Z":
            send_z(int(op[1]), int(op[2]), int(op[3]), True)
            return
        slot = int(op[1:])
        q, i = slot // NCH, slot % NCH
        if what == "Y":
            src = p_ref.at[pl.ds(TPS * s_of(slot, 1 - p), TPS)]
            remote(src, five_of(lefts[slot], rep), sy.at[slot], ry.at[slot], at_mate).start()
        elif what == "y":
            src = rows(rights[0][1], i)
            landed(src, ry.at[i])
            n = ORDER_OF_CHUNK[i]
            head = rights[0][1].at[pl.ds(CH * i, TPS)]
            pltpu.make_async_copy(head, five_of(lefts[n], mate), l_part.at[n]).start()
            to_sibling(p == 0, src, 0, 1, i)
        elif what == "p":
            n, f = (1, q) if q < 2 else (3, 1 if x == 3 else 0)
            src = rows(rights[n][f], i)
            landed(src, rplus.at[slot])
            if q < 2:
                to_sibling(p == 0, src, 1, q, i)
                to_sibling(p == 1, src, 0, q, i)
            else:
                to_sibling(p >= 0, src, 3, f, i)
        elif what == "m":
            n, f = (2, q) if q < 2 else (3, 0 if x == 3 else 1)
            src = rows(rights[n][f], i)
            landed(src, rminus.at[slot])
            to_sibling(p >= 0, src, n, f, i)
        elif what == "c":
            src = rows(four[q] if q < 2 else five, i)
            landed(src, rcross.at[slot])
            if q < 2:
                to_sibling(p == 1, src, 1, q, i)
        elif what == "P":
            if q < 2:
                src, dst = rows(four[q], i) if x == 3 else own(q, i), rights[1][q]
            elif x == 3:
                src, dst = rows(five, i), rights[3][0]
            else:
                f = 1 if x == 2 else 0
                src, dst = rows(rights[1][f], i), rights[3][f]
            remote(src, rows(dst, i), splus.at[slot], rplus.at[slot], at_plus).start()
        elif what == "M":
            if q < 2:
                src, dst = own(q, i) if x == 0 else rows(four[q], i), rights[2][q]
            elif x == 0:
                src, dst = rows(five, i), rights[3][0]
            else:
                src, dst = rows(rights[2][1], i), rights[3][1]
            remote(src, rows(dst, i), sminus.at[slot], rminus.at[slot], at_minus).start()
        else:
            if q < 2:
                src, dst = own(1 - q, i), four[q]
            else:
                src, dst = rows(rights[1][1] if x == 3 else rights[2][1], i), five
            remote(src, rows(dst, i), scross.at[slot], rcross.at[slot], at_cross).start()

    def sibling_op(op):
        what = op[0]
        if what == "B":
            i = int(op[1:])
            remote(rows(p_ref, i), rows(rights[0][1], i), sy.at[i], ry.at[i], at_mate).start()
        elif what == "y":
            n = int(op[1:])
            landed(five_of(lefts[n], mate), ry.at[n])
        elif what == "z":
            wait_z(int(op[1]), int(op[2]), int(op[3]))
        else:
            if op == FIRST_OF_SIBLING:
                pl.semaphore_wait(go, 1)
            send_z(int(op[1]), int(op[2]), int(op[3]), False)

    def prepare():
        for n in range(4):
            remote(meta_ref.at[s_of(n, 1 - p)], meta_in.at[n], smeta.at[n], rmeta.at[n], at_mate).start()
            pltpu.make_async_copy(meta_ref.at[s_of(n, p)], meta_sm.at[0, n], l_meta.at[0, n]).start()
        for n in range(4):
            src = p_ref.at[pl.ds(TPS * s_of(n, p), TPS)]
            pltpu.make_async_copy(src, five_of(lefts[n], rep), l_left.at[n]).start()

    def on_meta():
        for n in range(4):
            landed(meta_in.at[n], rmeta.at[n])
            pltpu.make_async_copy(meta_in.at[n], meta_sm.at[1, n], l_meta.at[1, n]).start()
        for q in range(2):
            for n in range(4):
                landed(meta_sm.at[q, n], l_meta.at[q, n])

    def multiply(n, q):
        total = out_ref if q == 0 else partial

        def slot(j, acc):
            a = lefts[n][meta_sm[q, n, 0, j]]
            b = rights[n][q][meta_sm[q, n, 1, j]]
            a_hi = a.astype(jnp.bfloat16)
            a_lo = (a - a_hi.astype(jnp.float32)).astype(jnp.bfloat16)
            b_hi = b.astype(jnp.bfloat16)
            b_lo = (b - b_hi.astype(jnp.float32)).astype(jnp.bfloat16)
            both = jnp.dot(
                jnp.concatenate([a_hi, a_lo], axis=1),
                jnp.concatenate(
                    [jnp.concatenate([b_hi, b_hi], axis=0), jnp.concatenate([b_lo, jnp.zeros_like(b_lo)], axis=0)], axis=1
                ),
                preferred_element_type=jnp.float32,
            )
            prod = both[:, :TILE] + both[:, TILE:]
            acc = prod + jnp.where(meta_sm[q, n, 2, j] > 0, acc, 0.0)
            sums[j] = acc
            return acc

        lax.fori_loop(0, NTASK, slot, jnp.zeros((TILE, TILE), jnp.float32), unroll=8)

        def collect(c, carry):
            got = jnp.where(meta_sm[q, n, 4, c] > 0, sums[meta_sm[q, n, 3, c]], 0.0)
            if n == 0:
                total[c] = got
            else:
                total[c] += got
            return carry

        lax.fori_loop(0, NC, collect, 0)

    def send_sums():
        for g in range(4):
            part = pl.ds(4 * g, 4)
            remote(partial.at[part], arrived.at[part], sc.at[g], rc.at[g], at_mate).start()

    def turns(order, segment, held):
        ready = set()
        for step, turn in enumerate(order):
            segment(step)
            if turn is None:
                send_sums()
                continue
            n, q = turn
            if not ready:
                on_meta()
            if n not in ready:
                ready.add(n)
                landed(five_of(lefts[n], rep), l_left.at[n])
                if held:
                    landed(five_of(lefts[n], mate), l_part.at[n])
            if not held:
                landed(rights[n][q], rd.at[2 * n + q])
            elif turn == (0, 0):
                landed(rights[0][0], l_own)
            multiply(n, q)
        segment(len(order))
        for g in range(4):
            part = pl.ds(4 * g, 4)
            landed(arrived.at[part], rc.at[g])
            out_ref[part] += arrived[part]

    @pl.when(holder)
    def _():
        def segment(step):
            for c in range(4):
                if SCHEDULE[c][step]:

                    @pl.when(x == c)
                    def _():
                        for op in SCHEDULE[c][step]:
                            holder_op(op, c)

        prepare()

        @pl.when(p == 0)
        def _():
            remote(p_ref, rights[0][0], sd.at[0], rd.at[0], at_sib).start()

        pltpu.make_async_copy(p_ref, rights[0][0], l_own).start()
        turns(HOLDER_TURNS, segment, True)

    @pl.when(jnp.logical_not(holder))
    def _():
        def segment(step):
            for op in SCHEDULE[4][step]:
                sibling_op(op)

        prepare()
        turns(SIBLING_TURNS, segment, False)

    for n in range(4):
        landed(meta_in.at[n], smeta.at[n])
        landed(partial.at[pl.ds(4 * n, 4)], sc.at[n])
        for kind in range(3):
            for side in range(2):
                landed(five_of(lefts[n], 0), sz.at[side, kind, n])

    @pl.when(holder)
    def _():
        for i in range(NCH):
            landed(five_of(lefts[0], 0), sy.at[i])
        for slot in range(3 * NCH):
            landed(rows(five, 0), splus.at[slot])
            landed(rows(five, 0), sminus.at[slot])
        for slot in range(2 * NCH):
            landed(rows(five, 0), scross.at[slot])

        @pl.when(jnp.logical_or(x == 0, x == 3))
        def _():
            for i in range(NCH):
                landed(rows(five, 0), scross.at[2 * NCH + i])

        for b in range(8):
            landed(five, sd.at[b])

    @pl.when(jnp.logical_not(holder))
    def _():
        for i in range(NCH):
            landed(rows(five, 0), sy.at[i])


def gather_and_multiply(p_tiles, meta):
    dma = pltpu.SemaphoreType.DMA
    block = pltpu.VMEM((NT, TILE, TILE), jnp.float32)
    target = pltpu.VMEM((NC, TILE, TILE), jnp.float32)
    return pl.pallas_call(
        kernel,
        out_shape=jax.ShapeDtypeStruct((NC, TILE, TILE), jnp.float32),
        in_specs=[pl.BlockSpec(memory_space=pl.ANY)] * 2,
        out_specs=pl.BlockSpec(memory_space=pltpu.VMEM),
        scratch_shapes=[block] * 15
        + [
            pltpu.VMEM((NTASK, TILE, TILE), jnp.float32),
            target,
            target,
            pltpu.VMEM((4, 8, 128), jnp.int32),
            pltpu.SMEM((2, 4, 8, 128), jnp.int32),
        ]
        + [dma((4,)), dma((12,)), dma((12,)), dma((12,)), dma((2, 3, 4)), dma((8,)), dma((4,)), dma((4,))] * 2
        + [dma, dma((4,)), dma((4,)), dma((2, 4)), pltpu.SemaphoreType.REGULAR],
        compiler_params=pltpu.CompilerParams(
            collective_id=0, has_side_effects=True, vmem_limit_bytes=60 * 1024 * 1024
        ),
    )(p_tiles, meta)


def per_device(p_tiles, tasks):
    own = p_tiles.reshape(NT, TILE, TILE)
    return gather_and_multiply(own, sort_tasks(tasks[0, 0]))[None, None]


def solution(mesh):
    return jax.shard_map(
        per_device,
        mesh=mesh,
        in_specs=(P("blk", "rep", None, None, None, None), P("blk", "rep", None, None, None)),
        out_specs=P("blk", "rep", None, None, None),
        check_vma=False,
    )
```

```python
import jax
import jax.numpy as jnp
from jax import lax
from jax.experimental import pallas as pl
from jax.experimental.pallas import tpu as pltpu
from jax.sharding import PartitionSpec as P

MESH = pl.DeviceIdType.MESH
TILE = 128
NT = 40
TPS = 5
NC = 16
NTASK = 48
CH = 10
NCH = NT // CH
ORDER_OF_CHUNK = (0, 1, 3, 2)

WAIT_MATE, WAIT_PLUS, WAIT_MINUS, WAIT_CROSS, WAIT_Z = 0, 1, 2, 3, 4
LEFT_TO_MATE, TO_PLUS, TO_MINUS, TO_CROSS, TO_Z, LET_SIBLING_GO, PANEL_TO_MATE = 5, 6, 7, 8, 9, 10, 11
SCHEDULE = (
    (
        (804, 600, 700, 805, 601, 701, 900, 912, 901, 913, 902, 914, 903, 915, 806, 412, 400, 908, 0, 304, 413, 401,
         604, 704, 904, 916, 909, 807, 414, 402, 910, 1, 305, 415, 403, 605, 705, 917, 204, 104, 808, 416, 408, 920,
         905, 404, 417, 2, 306, 921, 606, 706, 919, 1000, 105, 205, 809, 420, 409, 500, 501, 502, 911, 503, 3, 307,
         607, 707, 918, 421, 410, 208, 106, 602, 702, 907, 308),
        (419, 405, 923, 206, 107, 810, 603, 703, 906, 309, 418, 411, 922, 207, 100, 811, 800, 608, 708),
        (310, 423, 407, 209, 101, 801, 609, 709),
        (311, 422, 406, 210, 102, 802, 610, 710, 300),
        (211, 103, 803, 611, 711, 301),
        (),
        (200, 108, 302, 201, 109, 303),
        (202, 110, 203, 111),
        (),
        (),
    ),
    (
        (804, 600, 805, 601, 900, 912, 901, 913, 902, 914, 903, 915, 806, 412, 400, 908, 100, 0, 304, 413, 401, 604,
         904, 916, 704, 909, 807, 414, 402, 910, 1, 101, 305, 415, 403, 605, 917, 705, 204, 708, 800, 416, 408, 920,
         905, 404, 417, 2, 104, 306, 921, 606, 919, 706, 1000, 205, 801, 420, 409, 500, 501, 502, 911, 503, 3, 105,
         307, 607, 918, 707, 421, 410, 208, 602, 802, 907, 709, 106, 300),
        (419, 405, 923, 206, 603, 803, 906, 710, 107, 301, 418, 411, 922, 207, 608),
        (711, 302, 102, 423, 407, 209, 609),
        (700, 303, 103, 422, 406, 210, 610, 701, 108),
        (211, 611, 702, 109),
        (),
        (200, 703, 110, 201, 111),
        (202, 203),
        (),
        (),
    ),
    (
        (804, 600, 805, 601, 900, 912, 901, 913, 902, 914, 903, 915, 806, 412, 400, 908, 100, 0, 304, 413, 401, 604,
         904, 916, 704, 909, 807, 414, 402, 910, 1, 101, 305, 415, 403, 605, 917, 705, 204, 708, 800, 416, 408, 920,
         905, 404, 417, 2, 306, 104, 921, 606, 919, 706, 1000, 205, 801, 420, 409, 500, 501, 502, 911, 503, 3, 105,
         307, 607, 918, 707, 421, 410, 206, 608, 802, 907, 709, 106, 300),
        (419, 405, 923, 207, 609, 803, 906, 710, 107, 301, 418, 411, 922, 208, 610),
        (711, 102, 302, 423, 407, 209, 611),
        (700, 303, 103, 422, 406, 210, 602, 701, 108),
        (211, 603, 702, 109),
        (),
        (200, 703, 110, 201, 111),
        (202, 203),
        (),
        (),
    ),
    (
        (804, 805, 900, 912, 901, 913, 902, 914, 903, 915, 806, 412, 400, 908, 200, 100, 0, 304, 413, 401, 904, 916,
         604, 704, 909, 807, 414, 402, 910, 1, 201, 101, 305, 415, 403, 917, 605, 705, 800, 416, 408, 920, 905, 404,
         417, 2, 204, 104, 306, 921, 919, 606, 706, 1000, 801, 420, 409, 500, 501, 502, 911, 708, 503, 3, 205, 307,
         105, 918, 607, 707, 421, 410, 802, 907, 709, 206, 106, 300, 600),
        (419, 405, 923, 803, 906, 710, 107, 207, 301, 601, 418, 411, 922, 808),
        (711, 108, 302, 202, 602, 423, 407, 809),
        (700, 109, 303, 203, 603, 422, 406, 810, 701, 110, 308, 208, 608),
        (811, 702, 111, 309, 209, 609),
        (),
        (703, 102, 310, 210, 610, 103, 311, 211, 611),
        (),
        (),
        (),
    ),
    (
        (1100, 1101, 1102, 1103, 900, 912, 901, 913, 902, 914, 0, 412, 400, 1, 903, 915, 2, 413, 401, 3, 904, 916,
         414, 402, 917, 908, 905, 918, 415, 403, 906, 919, 909, 416, 404, 920, 907, 408, 417, 921, 910, 405, 418, 922,
         911, 406, 419, 923, 409, 420),
        (407, 421),
        (410, 422),
        (411, 423),
        (),
        (),
        (),
        (),
        (),
        (),
    ),
)
HOLDER_TURNS = ((0, 1), (0, 0), (1, 1), (2, 1), (3, 1), None, (1, 0), (2, 0), (3, 0))
SIBLING_TURNS = ((0, 1), (1, 1), (2, 1), (3, 1), None, (0, 0), (1, 0), (2, 0), (3, 0))


FIRST_OF_SIBLING = next(op for segment in SCHEDULE[4] for op in segment if op // 100 == TO_Z)


def sort_tasks(tasks):
    left, right, target = tasks[:, 0], tasks[:, 1], tasks[:, 2]
    slots = jnp.arange(NTASK, dtype=jnp.int32)
    before = (target[:, None, :] < target[:, :, None]) | (
        (target[:, None, :] == target[:, :, None]) & (slots[None, None, :] < slots[None, :, None])
    )
    rank = jnp.sum(before.astype(jnp.int32), axis=2)
    place = (rank[:, :, None] == slots[None, None, :]).astype(jnp.int32)
    pick = lambda v: jnp.sum(place * v[:, :, None], axis=1)
    sorted_target = pick(target)
    same = jnp.concatenate(
        [jnp.zeros_like(target[:, :1]), (sorted_target[:, 1:] == sorted_target[:, :-1]).astype(jnp.int32)], axis=1
    )
    cols = jnp.arange(NC, dtype=jnp.int32)
    count = jnp.sum((target[:, :, None] == cols).astype(jnp.int32), axis=1)
    upto = jnp.sum((target[:, :, None] <= cols).astype(jnp.int32), axis=1)
    last = jnp.maximum(upto - 1, 0)
    wide = lambda v: jnp.pad(v, ((0, 0), (0, 128 - v.shape[1])))
    rows = [wide(jnp.clip(pick(left), 0, NT - 1)), wide(jnp.clip(pick(right), 0, NT - 1)), wide(same), wide(last)]
    rows.append(wide((count > 0).astype(jnp.int32)))
    rows += [jnp.zeros_like(rows[0])] * 3
    return jnp.stack(rows, axis=1)


def kernel(p_ref, meta_ref, out_ref, *scratch):
    lefts = scratch[0:4]
    rights = (scratch[4:6], scratch[6:8], scratch[8:10], scratch[10:12])
    four = scratch[12:14]
    (five, sums, partial, arrived, meta_in, meta_sm) = scratch[14:20]
    (ry, rplus, rminus, rcross, rz, rd, rmeta, rc) = scratch[20:28]
    (sy, splus, sminus, scross, sz, sd, smeta, sc) = scratch[28:36]
    (l_own, l_left, l_part, l_meta, go) = scratch[36:41]

    blk, rep = lax.axis_index("blk"), lax.axis_index("rep")
    h, x, k = blk // 8, (blk % 8) // 2, blk % 2
    z, lo = rep // 2, rep % 2
    p = (lo + h) % 2
    holder = k == p
    mate = rep + 1 - 2 * lo
    at_plus = (h * 8 + ((x + 1) % 4) * 2 + k, rep)
    at_minus = (h * 8 + ((x + 3) % 4) * 2 + k, rep)
    at_mate = (blk, mate)
    at_cross = ((1 - h) * 8 + x * 2 + k, mate)
    at_zp = (blk, ((z + 1) % 4) * 2 + lo)
    at_zm = (blk, ((z + 3) % 4) * 2 + lo)
    at_sib = (blk + 1 - 2 * k, rep)

    def s_of(n, parity):
        odd = (k + parity) % 2
        f = (1 - k) * parity
        return odd + (0, 2, 6, 4)[n] + f * (0, 4, -2, -2)[n]

    barrier = pltpu.get_barrier_semaphore()
    for peer in (at_plus, at_minus, at_mate, at_cross, at_zp, at_zm, at_sib):
        pl.semaphore_signal(barrier, inc=1, device_id=peer, device_id_type=MESH)
    pl.semaphore_wait(barrier, 7)

    def remote(src, dst, ssem, rsem, peer):
        return pltpu.make_async_remote_copy(
            src_ref=src, dst_ref=dst, send_sem=ssem, recv_sem=rsem, device_id=peer, device_id_type=MESH
        )

    def rows(ref, i):
        return ref.at[pl.ds(CH * i, CH)]

    def five_of(ref, r):
        return ref.at[pl.ds(TPS * r, TPS)]

    def landed(ref, sem):
        pltpu.make_async_copy(ref, ref, sem).wait()

    def own(q, i):
        return rows(p_ref, i) if q == 0 else rows(rights[0][1], i)

    def to_sibling(here, src, n, q, i):
        @pl.when(here)
        def _():
            remote(src, rows(rights[n][q], i), sd.at[2 * n + q], rd.at[2 * n + q], at_sib).start()

    def sliver_of(side, kind):
        away = (z + 2) % 4 if kind == 2 else (z + 3) % 4 if side == 0 else (z + 1) % 4
        return away * 2 + (lo if kind == 0 or (kind == 2 and side == 0) else 1 - lo)

    def wait_z(side, kind, n):
        landed(five_of(lefts[n], sliver_of(side, kind)), rz.at[side, kind, n])

    def send_z(side, kind, n, held):
        if kind == 0:
            src, r = p_ref.at[pl.ds(TPS * s_of(n, p), TPS)], rep
        elif kind == 1:
            r = mate
            src = rights[0][1].at[pl.ds(CH * ORDER_OF_CHUNK[n], TPS)] if held else five_of(lefts[n], r)
        else:
            r = sliver_of(side, side)
            src = five_of(lefts[n], r)
        peer = (at_zp, at_zm)[side]
        remote(src, five_of(lefts[n], r), sz.at[side, kind, n], rz.at[side, kind, n], peer).start()

    def along_z(slot):
        return slot // 12, slot % 12 // 4, slot % 4

    def holder_op(op, x):
        what, slot = divmod(op, 100)
        if what == LET_SIBLING_GO:
            pl.semaphore_signal(go, inc=1, device_id=at_sib, device_id_type=MESH)
            return
        if what == WAIT_Z:
            wait_z(*along_z(slot))
            return
        if what == TO_Z:
            send_z(*along_z(slot), True)
            return
        q, i = slot // NCH, slot % NCH
        if what == LEFT_TO_MATE:
            src = p_ref.at[pl.ds(TPS * s_of(slot, 1 - p), TPS)]
            remote(src, five_of(lefts[slot], rep), sy.at[slot], ry.at[slot], at_mate).start()
        elif what == WAIT_MATE:
            src = rows(rights[0][1], i)
            landed(src, ry.at[i])
            n = ORDER_OF_CHUNK[i]
            head = rights[0][1].at[pl.ds(CH * i, TPS)]
            pltpu.make_async_copy(head, five_of(lefts[n], mate), l_part.at[n]).start()
            to_sibling(p == 0, src, 0, 1, i)
        elif what == WAIT_PLUS:
            n, f = (1, q) if q < 2 else (3, 1 if x == 3 else 0)
            src = rows(rights[n][f], i)
            landed(src, rplus.at[slot])
            if q < 2:
                to_sibling(p == 0, src, 1, q, i)
                to_sibling(p == 1, src, 0, q, i)
            else:
                to_sibling(p >= 0, src, 3, f, i)
        elif what == WAIT_MINUS:
            n, f = (2, q) if q < 2 else (3, 0 if x == 3 else 1)
            src = rows(rights[n][f], i)
            landed(src, rminus.at[slot])
            to_sibling(p >= 0, src, n, f, i)
        elif what == WAIT_CROSS:
            src = rows(four[q] if q < 2 else five, i)
            landed(src, rcross.at[slot])
            if q < 2:
                to_sibling(p == 1, src, 1, q, i)
        elif what == TO_PLUS:
            if q < 2:
                src, dst = rows(four[q], i) if x == 3 else own(q, i), rights[1][q]
            elif x == 3:
                src, dst = rows(five, i), rights[3][0]
            else:
                f = 1 if x == 2 else 0
                src, dst = rows(rights[1][f], i), rights[3][f]
            remote(src, rows(dst, i), splus.at[slot], rplus.at[slot], at_plus).start()
        elif what == TO_MINUS:
            if q < 2:
                src, dst = own(q, i) if x == 0 else rows(four[q], i), rights[2][q]
            elif x == 0:
                src, dst = rows(five, i), rights[3][0]
            else:
                src, dst = rows(rights[2][1], i), rights[3][1]
            remote(src, rows(dst, i), sminus.at[slot], rminus.at[slot], at_minus).start()
        else:
            if q < 2:
                src, dst = own(1 - q, i), four[q]
            else:
                src, dst = rows(rights[1][1] if x == 3 else rights[2][1], i), five
            remote(src, rows(dst, i), scross.at[slot], rcross.at[slot], at_cross).start()

    def sibling_op(op):
        what, slot = divmod(op, 100)
        if what == PANEL_TO_MATE:
            i = slot
            remote(rows(p_ref, i), rows(rights[0][1], i), sy.at[i], ry.at[i], at_mate).start()
        elif what == WAIT_MATE:
            landed(five_of(lefts[slot], mate), ry.at[slot])
        elif what == WAIT_Z:
            wait_z(*along_z(slot))
        else:
            if op == FIRST_OF_SIBLING:
                pl.semaphore_wait(go, 1)
            send_z(*along_z(slot), False)

    def prepare():
        for n in range(4):
            remote(meta_ref.at[s_of(n, 1 - p)], meta_in.at[n], smeta.at[n], rmeta.at[n], at_mate).start()
            pltpu.make_async_copy(meta_ref.at[s_of(n, p)], meta_sm.at[0, n], l_meta.at[0, n]).start()
        for n in range(4):
            src = p_ref.at[pl.ds(TPS * s_of(n, p), TPS)]
            pltpu.make_async_copy(src, five_of(lefts[n], rep), l_left.at[n]).start()

    def on_meta():
        for n in range(4):
            landed(meta_in.at[n], rmeta.at[n])
            pltpu.make_async_copy(meta_in.at[n], meta_sm.at[1, n], l_meta.at[1, n]).start()
        for q in range(2):
            for n in range(4):
                landed(meta_sm.at[q, n], l_meta.at[q, n])

    def multiply(n, q):
        total = out_ref if q == 0 else partial

        def slot(j, acc):
            a = lefts[n][meta_sm[q, n, 0, j]]
            b = rights[n][q][meta_sm[q, n, 1, j]]
            a_hi = a.astype(jnp.bfloat16)
            a_lo = (a - a_hi.astype(jnp.float32)).astype(jnp.bfloat16)
            b_hi = b.astype(jnp.bfloat16)
            b_lo = (b - b_hi.astype(jnp.float32)).astype(jnp.bfloat16)
            both = jnp.dot(
                jnp.concatenate([a_hi, a_lo], axis=1),
                jnp.concatenate(
                    [jnp.concatenate([b_hi, b_hi], axis=0), jnp.concatenate([b_lo, jnp.zeros_like(b_lo)], axis=0)], axis=1
                ),
                preferred_element_type=jnp.float32,
            )
            prod = both[:, :TILE] + both[:, TILE:]
            acc = prod + jnp.where(meta_sm[q, n, 2, j] > 0, acc, 0.0)
            sums[j] = acc
            return acc

        lax.fori_loop(0, NTASK, slot, jnp.zeros((TILE, TILE), jnp.float32), unroll=8)

        def collect(c, carry):
            got = jnp.where(meta_sm[q, n, 4, c] > 0, sums[meta_sm[q, n, 3, c]], 0.0)
            if n == 0:
                total[c] = got
            else:
                total[c] += got
            return carry

        lax.fori_loop(0, NC, collect, 0)

    def send_sums():
        for g in range(4):
            part = pl.ds(4 * g, 4)
            remote(partial.at[part], arrived.at[part], sc.at[g], rc.at[g], at_mate).start()

    def turns(order, segment, held):
        ready = set()
        for step, turn in enumerate(order):
            segment(step)
            if turn is None:
                send_sums()
                continue
            n, q = turn
            if not ready:
                on_meta()
            if n not in ready:
                ready.add(n)
                landed(five_of(lefts[n], rep), l_left.at[n])
                if held:
                    landed(five_of(lefts[n], mate), l_part.at[n])
            if not held:
                landed(rights[n][q], rd.at[2 * n + q])
            elif turn == (0, 0):
                landed(rights[0][0], l_own)
            multiply(n, q)
        segment(len(order))
        for g in range(4):
            part = pl.ds(4 * g, 4)
            landed(arrived.at[part], rc.at[g])
            out_ref[part] += arrived[part]

    @pl.when(holder)
    def _():
        def segment(step):
            for c in range(4):
                if SCHEDULE[c][step]:

                    @pl.when(x == c)
                    def _():
                        for op in SCHEDULE[c][step]:
                            holder_op(op, c)

        prepare()

        @pl.when(p == 0)
        def _():
            remote(p_ref, rights[0][0], sd.at[0], rd.at[0], at_sib).start()

        pltpu.make_async_copy(p_ref, rights[0][0], l_own).start()
        turns(HOLDER_TURNS, segment, True)

    @pl.when(jnp.logical_not(holder))
    def _():
        def segment(step):
            for op in SCHEDULE[4][step]:
                sibling_op(op)

        prepare()
        turns(SIBLING_TURNS, segment, False)

    for n in range(4):
        landed(meta_in.at[n], smeta.at[n])
        landed(partial.at[pl.ds(4 * n, 4)], sc.at[n])
        for kind in range(3):
            for side in range(2):
                landed(five_of(lefts[n], 0), sz.at[side, kind, n])

    @pl.when(holder)
    def _():
        for i in range(NCH):
            landed(five_of(lefts[0], 0), sy.at[i])
        for slot in range(3 * NCH):
            landed(rows(five, 0), splus.at[slot])
            landed(rows(five, 0), sminus.at[slot])
        for slot in range(2 * NCH):
            landed(rows(five, 0), scross.at[slot])

        @pl.when(jnp.logical_or(x == 0, x == 3))
        def _():
            for i in range(NCH):
                landed(rows(five, 0), scross.at[2 * NCH + i])

        for b in range(8):
            landed(five, sd.at[b])

    @pl.when(jnp.logical_not(holder))
    def _():
        for i in range(NCH):
            landed(rows(five, 0), sy.at[i])


def gather_and_multiply(p_tiles, meta):
    dma = pltpu.SemaphoreType.DMA
    block = pltpu.VMEM((NT, TILE, TILE), jnp.float32)
    target = pltpu.VMEM((NC, TILE, TILE), jnp.float32)
    return pl.pallas_call(
        kernel,
        out_shape=jax.ShapeDtypeStruct((NC, TILE, TILE), jnp.float32),
        in_specs=[pl.BlockSpec(memory_space=pl.ANY)] * 2,
        out_specs=pl.BlockSpec(memory_space=pltpu.VMEM),
        scratch_shapes=[block] * 15
        + [
            pltpu.VMEM((NTASK, TILE, TILE), jnp.float32),
            target,
            target,
            pltpu.VMEM((4, 8, 128), jnp.int32),
            pltpu.SMEM((2, 4, 8, 128), jnp.int32),
        ]
        + [dma((4,)), dma((12,)), dma((12,)), dma((12,)), dma((2, 3, 4)), dma((8,)), dma((4,)), dma((4,))] * 2
        + [dma, dma((4,)), dma((4,)), dma((2, 4)), pltpu.SemaphoreType.REGULAR],
        compiler_params=pltpu.CompilerParams(
            collective_id=0, has_side_effects=True, vmem_limit_bytes=60 * 1024 * 1024
        ),
    )(p_tiles, meta)


def per_device(p_tiles, tasks):
    own = p_tiles.reshape(NT, TILE, TILE)
    return gather_and_multiply(own, sort_tasks(tasks[0, 0]))[None, None]


def solution(mesh):
    return jax.shard_map(
        per_device,
        mesh=mesh,
        in_specs=(P("blk", "rep", None, None, None, None), P("blk", "rep", None, None, None)),
        out_specs=P("blk", "rep", None, None, None),
        check_vma=False,
    )
```

```python
import jax
import jax.numpy as jnp
from jax import lax
from jax.experimental import pallas as pl
from jax.experimental.pallas import tpu as pltpu
from jax.sharding import PartitionSpec as P

MESH = pl.DeviceIdType.MESH
TILE = 128
NT = 40
TPS = 5
NC = 16
NTASK = 48
CH = 10
NCH = NT // CH
ORDER_OF_CHUNK = (0, 1, 3, 2)

WAIT_MATE, WAIT_PLUS, WAIT_MINUS, WAIT_CROSS, WAIT_Z = 0, 1, 2, 3, 4
LEFT_TO_MATE, TO_PLUS, TO_MINUS, TO_CROSS, TO_Z, LET_SIBLING_GO, PANEL_TO_MATE = 5, 6, 7, 8, 9, 10, 11
SCHEDULE = (
    (
        (804, 600, 700, 805, 601, 701, 900, 912, 901, 913, 902, 914, 903, 915, 806, 412, 400, 908, 0, 304, 413, 401,
         604, 704, 904, 916, 909, 807, 414, 402, 910, 1, 305, 415, 403, 605, 705, 917, 204, 104, 808, 416, 408, 920,
         905, 404, 417, 2, 306, 921, 606, 706, 919, 1000, 105, 205, 809, 420, 409, 500, 501, 502, 911, 503, 3, 307,
         607, 707, 918, 421, 410, 208, 106, 602, 702, 907, 308),
        (419, 405, 923, 206, 107, 810, 603, 703, 906, 309, 418, 411, 922, 207, 100, 811, 800, 608, 708),
        (310, 423, 407, 209, 101, 801, 609, 709),
        (311, 422, 406, 210, 102, 802, 610, 710, 300),
        (211, 103, 803, 611, 711, 301),
        (),
        (200, 108, 302, 201, 109, 303),
        (202, 110, 203, 111),
        (),
        (),
    ),
    (
        (804, 600, 805, 601, 900, 912, 901, 913, 902, 914, 903, 915, 806, 412, 400, 908, 100, 0, 304, 413, 401, 604,
         904, 916, 704, 909, 807, 414, 402, 910, 1, 101, 305, 415, 403, 605, 917, 705, 204, 708, 800, 416, 408, 920,
         905, 404, 417, 2, 104, 306, 921, 606, 919, 706, 1000, 205, 801, 420, 409, 500, 501, 502, 911, 503, 3, 105,
         307, 607, 918, 707, 421, 410, 208, 602, 802, 907, 709, 106, 300),
        (419, 405, 923, 206, 603, 803, 906, 710, 107, 301, 418, 411, 922, 207, 608),
        (711, 302, 102, 423, 407, 209, 609),
        (700, 303, 103, 422, 406, 210, 610, 701, 108),
        (211, 611, 702, 109),
        (),
        (200, 703, 110, 201, 111),
        (202, 203),
        (),
        (),
    ),
    (
        (804, 600, 805, 601, 900, 912, 901, 913, 902, 914, 903, 915, 806, 412, 400, 908, 100, 0, 304, 413, 401, 604,
         904, 916, 704, 909, 807, 414, 402, 910, 1, 101, 305, 415, 403, 605, 917, 705, 204, 708, 800, 416, 408, 920,
         905, 404, 417, 2, 306, 104, 921, 606, 919, 706, 1000, 205, 801, 420, 409, 500, 501, 502, 911, 503, 3, 105,
         307, 607, 918, 707, 421, 410, 206, 608, 802, 907, 709, 106, 300),
        (419, 405, 923, 207, 609, 803, 906, 710, 107, 301, 418, 411, 922, 208, 610),
        (711, 102, 302, 423, 407, 209, 611),
        (700, 303, 103, 422, 406, 210, 602, 701, 108),
        (211, 603, 702, 109),
        (),
        (200, 703, 110, 201, 111),
        (202, 203),
        (),
        (),
    ),
    (
        (804, 805, 900, 912, 901, 913, 902, 914, 903, 915, 806, 412, 400, 908, 200, 100, 0, 304, 413, 401, 904, 916,
         604, 704, 909, 807, 414, 402, 910, 1, 201, 101, 305, 415, 403, 917, 605, 705, 800, 416, 408, 920, 905, 404,
         417, 2, 204, 104, 306, 921, 919, 606, 706, 1000, 801, 420, 409, 500, 501, 502, 911, 708, 503, 3, 205, 307,
         105, 918, 607, 707, 421, 410, 802, 907, 709, 206, 106, 300, 600),
        (419, 405, 923, 803, 906, 710, 107, 207, 301, 601, 418, 411, 922, 808),
        (711, 108, 302, 202, 602, 423, 407, 809),
        (700, 109, 303, 203, 603, 422, 406, 810, 701, 110, 308, 208, 608),
        (811, 702, 111, 309, 209, 609),
        (),
        (703, 102, 310, 210, 610, 103, 311, 211, 611),
        (),
        (),
        (),
    ),
    (
        (1100, 1101, 1102, 1103, 900, 912, 901, 913, 902, 914, 0, 412, 400, 1, 903, 915, 2, 413, 401, 3, 904, 916,
         414, 402, 917, 908, 905, 918, 415, 403, 906, 919, 909, 416, 404, 920, 907, 408, 417, 921, 910, 405, 418, 922,
         911, 406, 419, 923, 409, 420),
        (407, 421),
        (410, 422),
        (411, 423),
        (),
        (),
        (),
        (),
        (),
        (),
    ),
)
HOLDER_TURNS = ((0, 1), (0, 0), (1, 1), (2, 1), (3, 1), None, (1, 0), (2, 0), (3, 0))
SIBLING_TURNS = ((0, 1), (1, 1), (2, 1), (3, 1), None, (0, 0), (1, 0), (2, 0), (3, 0))


MIDDLE = 8
FIRST_OF_SIBLING = next(op for segment in SCHEDULE[4] for op in segment if op // 100 == TO_Z)


def sort_tasks(tasks_ref, meta_ref):
    down = lax.broadcasted_iota(jnp.int32, (NTASK, NTASK), 0)
    along = lax.broadcasted_iota(jnp.int32, (NTASK, NTASK), 1)

    def turned(row):
        return jnp.sum(jnp.where(down == along, row, 0), axis=1, keepdims=True)

    for step in range(tasks_ref.shape[1]):
        row = lambda f: jnp.broadcast_to(tasks_ref[f, step : step + 1, :], (NTASK, NTASK))
        target = row(2)
        left, right, mine = turned(row(0)), turned(row(1)), turned(target)
        before = jnp.logical_or(target < mine, jnp.logical_and(target == mine, along < down))
        rank = jnp.sum(jnp.where(before, 1, 0), axis=1, keepdims=True)
        pick = lambda column, place: jnp.sum(jnp.where(rank == place, column, 0), axis=0, keepdims=True)
        here, ahead = pick(mine, along), pick(mine, along - 1)
        same = jnp.where(jnp.logical_and(here == ahead, along[:1] > 0), 1, 0)
        upto = jnp.sum(jnp.where(mine <= along, 1, 0), axis=0, keepdims=True)
        count = jnp.sum(jnp.where(mine == along, 1, 0), axis=0, keepdims=True)
        rows = (jnp.clip(pick(left, along), 0, NT - 1), jnp.clip(pick(right, along), 0, NT - 1), same)
        rows += (jnp.maximum(upto - 1, 0), jnp.where(count > 0, 1, 0))
        for f, v in enumerate(rows):
            meta_ref[step, f : f + 1, :NTASK] = v


def kernel(p_ref, tasks_ref, out_ref, *scratch):
    lefts = scratch[0:4]
    rights = (scratch[4:6], scratch[6:8], scratch[8:10], scratch[10:12])
    four = scratch[12:14]
    (five, sums, partial, arrived, meta_in, meta_sm) = scratch[14:20]
    (ry, rplus, rminus, rcross, rz, rd, rmeta, rc) = scratch[20:28]
    (sy, splus, sminus, scross, sz, sd, smeta, sc) = scratch[28:36]
    (l_own, l_left, l_part, l_meta, go, meta_ref) = scratch[36:42]

    blk, rep = lax.axis_index("blk"), lax.axis_index("rep")
    h, x, k = blk // 8, (blk % 8) // 2, blk % 2
    z, lo = rep // 2, rep % 2
    p = (lo + h) % 2
    holder = k == p
    mate = rep + 1 - 2 * lo
    at_plus = (h * 8 + ((x + 1) % 4) * 2 + k, rep)
    at_minus = (h * 8 + ((x + 3) % 4) * 2 + k, rep)
    at_mate = (blk, mate)
    at_cross = ((1 - h) * 8 + x * 2 + k, mate)
    at_zp = (blk, ((z + 1) % 4) * 2 + lo)
    at_zm = (blk, ((z + 3) % 4) * 2 + lo)
    at_sib = (blk + 1 - 2 * k, rep)

    def s_of(n, parity):
        odd = (k + parity) % 2
        f = (1 - k) * parity
        return odd + (0, 2, 6, 4)[n] + f * (0, 4, -2, -2)[n]

    barrier = pltpu.get_barrier_semaphore()
    for peer in (at_plus, at_minus, at_mate, at_cross, at_zp, at_zm, at_sib):
        pl.semaphore_signal(barrier, inc=1, device_id=peer, device_id_type=MESH)
    pl.semaphore_wait(barrier, 7)

    def remote(src, dst, ssem, rsem, peer):
        return pltpu.make_async_remote_copy(
            src_ref=src, dst_ref=dst, send_sem=ssem, recv_sem=rsem, device_id=peer, device_id_type=MESH
        )

    def rows(ref, i):
        return ref.at[pl.ds(CH * i, CH)]

    def five_of(ref, r):
        return ref.at[pl.ds(TPS * r, TPS)]

    def landed(ref, sem):
        pltpu.make_async_copy(ref, ref, sem).wait()

    def own(q, i):
        return rows(p_ref, i) if q == 0 else rows(rights[0][1], i)

    def to_sibling(here, src, n, q, i):
        @pl.when(here)
        def _():
            remote(src, rows(rights[n][q], i), sd.at[2 * n + q], rd.at[2 * n + q], at_sib).start()

    def sliver_of(side, kind):
        away = (z + 2) % 4 if kind == 2 else (z + 3) % 4 if side == 0 else (z + 1) % 4
        return away * 2 + (lo if kind == 0 or (kind == 2 and side == 0) else 1 - lo)

    def wait_z(side, kind, n):
        landed(five_of(lefts[n], sliver_of(side, kind)), rz.at[side, kind, n])

    def send_z(side, kind, n, held):
        if kind == 0:
            src, r = p_ref.at[pl.ds(TPS * s_of(n, p), TPS)], rep
        elif kind == 1:
            r = mate
            src = rights[0][1].at[pl.ds(CH * ORDER_OF_CHUNK[n], TPS)] if held else five_of(lefts[n], r)
        else:
            r = sliver_of(side, side)
            src = five_of(lefts[n], r)
        peer = (at_zp, at_zm)[side]
        remote(src, five_of(lefts[n], r), sz.at[side, kind, n], rz.at[side, kind, n], peer).start()

    def along_z(slot):
        return slot // 12, slot % 12 // 4, slot % 4

    def holder_op(op, x):
        what, slot = divmod(op, 100)
        if what == LET_SIBLING_GO:
            pl.semaphore_signal(go, inc=1, device_id=at_sib, device_id_type=MESH)
            return
        if what == WAIT_Z:
            wait_z(*along_z(slot))
            return
        if what == TO_Z:
            send_z(*along_z(slot), True)
            return
        q, i = slot // NCH, slot % NCH
        if what == LEFT_TO_MATE:
            src = p_ref.at[pl.ds(TPS * s_of(slot, 1 - p), TPS)]
            remote(src, five_of(lefts[slot], rep), sy.at[slot], ry.at[slot], at_mate).start()
        elif what == WAIT_MATE:
            src = rows(rights[0][1], i)
            landed(src, ry.at[i])
            n = ORDER_OF_CHUNK[i]
            head = rights[0][1].at[pl.ds(CH * i, TPS)]
            pltpu.make_async_copy(head, five_of(lefts[n], mate), l_part.at[n]).start()
            to_sibling(p == 0, src, 0, 1, i)
        elif what == WAIT_PLUS:
            n, f = (1, q) if q < 2 else (3, 1 if x == 3 else 0)
            src = rows(rights[n][f], i)
            landed(src, rplus.at[slot])
            if q < 2:
                to_sibling(p == 0, src, 1, q, i)
                to_sibling(p == 1, src, 0, q, i)
            else:
                to_sibling(p >= 0, src, 3, f, i)
        elif what == WAIT_MINUS:
            n, f = (2, q) if q < 2 else (3, 0 if x == 3 else 1)
            src = rows(rights[n][f], i)
            landed(src, rminus.at[slot])
            to_sibling(p >= 0, src, n, f, i)
        elif what == WAIT_CROSS:
            src = rows(four[q] if q < 2 else five, i)
            landed(src, rcross.at[slot])
            if q < 2:
                to_sibling(p == 1, src, 1, q, i)
        elif what == TO_PLUS:
            if q < 2:
                src, dst = rows(four[q], i) if x == 3 else own(q, i), rights[1][q]
            elif x == 3:
                src, dst = rows(five, i), rights[3][0]
            else:
                f = 1 if x == 2 else 0
                src, dst = rows(rights[1][f], i), rights[3][f]
            remote(src, rows(dst, i), splus.at[slot], rplus.at[slot], at_plus).start()
        elif what == TO_MINUS:
            if q < 2:
                src, dst = own(q, i) if x == 0 else rows(four[q], i), rights[2][q]
            elif x == 0:
                src, dst = rows(five, i), rights[3][0]
            else:
                src, dst = rows(rights[2][1], i), rights[3][1]
            remote(src, rows(dst, i), sminus.at[slot], rminus.at[slot], at_minus).start()
        else:
            if q < 2:
                src, dst = own(1 - q, i), four[q]
            else:
                src, dst = rows(rights[1][1] if x == 3 else rights[2][1], i), five
            remote(src, rows(dst, i), scross.at[slot], rcross.at[slot], at_cross).start()

    def sibling_op(op):
        what, slot = divmod(op, 100)
        if what == PANEL_TO_MATE:
            i = slot
            remote(rows(p_ref, i), rows(rights[0][1], i), sy.at[i], ry.at[i], at_mate).start()
        elif what == WAIT_MATE:
            landed(five_of(lefts[slot], mate), ry.at[slot])
        elif what == WAIT_Z:
            wait_z(*along_z(slot))
        else:
            if op == FIRST_OF_SIBLING:
                pl.semaphore_wait(go, 1)
            send_z(*along_z(slot), False)

    def keep_left():
        for n in range(4):
            src = p_ref.at[pl.ds(TPS * s_of(n, p), TPS)]
            pltpu.make_async_copy(src, five_of(lefts[n], rep), l_left.at[n]).start()

    def send_meta():
        for n in range(4):
            remote(meta_ref.at[s_of(n, 1 - p)], meta_in.at[n], smeta.at[n], rmeta.at[n], at_mate).start()
            pltpu.make_async_copy(meta_ref.at[s_of(n, p)], meta_sm.at[0, n], l_meta.at[0, n]).start()

    def on_meta():
        for n in range(4):
            landed(meta_in.at[n], rmeta.at[n])
            pltpu.make_async_copy(meta_in.at[n], meta_sm.at[1, n], l_meta.at[1, n]).start()
        for q in range(2):
            for n in range(4):
                landed(meta_sm.at[q, n], l_meta.at[q, n])

    def multiply(n, q):
        total = out_ref if q == 0 else partial

        def slot(j, acc):
            a = lefts[n][meta_sm[q, n, 0, j]]
            b = rights[n][q][meta_sm[q, n, 1, j]]
            a_hi = a.astype(jnp.bfloat16)
            a_lo = (a - a_hi.astype(jnp.float32)).astype(jnp.bfloat16)
            b_hi = b.astype(jnp.bfloat16)
            b_lo = (b - b_hi.astype(jnp.float32)).astype(jnp.bfloat16)
            both = jnp.dot(
                jnp.concatenate([a_hi, a_lo], axis=1),
                jnp.concatenate(
                    [jnp.concatenate([b_hi, b_hi], axis=0), jnp.concatenate([b_lo, jnp.zeros_like(b_lo)], axis=0)], axis=1
                ),
                preferred_element_type=jnp.float32,
            )
            prod = both[:, :TILE] + both[:, TILE:]
            acc = prod + jnp.where(meta_sm[q, n, 2, j] > 0, acc, 0.0)
            sums[j] = acc
            return acc

        lax.fori_loop(0, NTASK, slot, jnp.zeros((TILE, TILE), jnp.float32), unroll=16)

        def collect(c, carry):
            got = jnp.where(meta_sm[q, n, 4, c] > 0, sums[meta_sm[q, n, 3, c]], 0.0)
            if n == 0:
                total[c] = got
            else:
                total[c] += got
            return carry

        lax.fori_loop(0, NC, collect, 0)

    def send_sums():
        for g in range(4):
            part = pl.ds(4 * g, 4)
            remote(partial.at[part], arrived.at[part], sc.at[g], rc.at[g], at_mate).start()

    def turns(order, segment, held):
        ready = set()
        segment(0, None, 0)
        sort_tasks(tasks_ref, meta_ref)
        segment(0, 0, MIDDLE)
        send_meta()
        for step, turn in enumerate(order):
            segment(step, 0 if step else MIDDLE, None)
            if turn is None:
                send_sums()
                continue
            n, q = turn
            if not ready:
                on_meta()
            if n not in ready:
                ready.add(n)
                landed(five_of(lefts[n], rep), l_left.at[n])
                if held:
                    landed(five_of(lefts[n], mate), l_part.at[n])
            if not held:
                landed(rights[n][q], rd.at[2 * n + q])
            elif turn == (0, 0):
                landed(rights[0][0], l_own)
            multiply(n, q)
        segment(len(order), 0, None)
        for g in range(4):
            part = pl.ds(4 * g, 4)
            landed(arrived.at[part], rc.at[g])
            out_ref[part] += arrived[part]

    def part_of(c, step, begin, end):
        entries = SCHEDULE[c][step]
        first = 0
        if step == 0:
            first = next(i for i, op in enumerate(entries) if op // 100 <= WAIT_Z or (c == 4 and op // 100 == TO_Z))
        return entries[0 if begin is None else first + begin : None if end is None else first + end]

    @pl.when(holder)
    def _():
        def segment(step, begin, end):
            for c in range(4):
                ops = part_of(c, step, begin, end)
                if ops:

                    @pl.when(x == c)
                    def _():
                        for op in ops:
                            holder_op(op, c)

            if begin is None:
                keep_left()

                @pl.when(p == 0)
                def _():
                    remote(p_ref, rights[0][0], sd.at[0], rd.at[0], at_sib).start()

                pltpu.make_async_copy(p_ref, rights[0][0], l_own).start()

        turns(HOLDER_TURNS, segment, True)

    @pl.when(jnp.logical_not(holder))
    def _():
        def segment(step, begin, end):
            for op in part_of(4, step, begin, end):
                sibling_op(op)
            if begin is None:
                keep_left()

        turns(SIBLING_TURNS, segment, False)

    for n in range(4):
        landed(meta_in.at[n], smeta.at[n])
        landed(partial.at[pl.ds(4 * n, 4)], sc.at[n])
        for kind in range(3):
            for side in range(2):
                landed(five_of(lefts[n], 0), sz.at[side, kind, n])

    @pl.when(holder)
    def _():
        for i in range(NCH):
            landed(five_of(lefts[0], 0), sy.at[i])
        for slot in range(3 * NCH):
            landed(rows(five, 0), splus.at[slot])
            landed(rows(five, 0), sminus.at[slot])
        for slot in range(2 * NCH):
            landed(rows(five, 0), scross.at[slot])

        @pl.when(jnp.logical_or(x == 0, x == 3))
        def _():
            for i in range(NCH):
                landed(rows(five, 0), scross.at[2 * NCH + i])

        for b in range(8):
            landed(five, sd.at[b])

    @pl.when(jnp.logical_not(holder))
    def _():
        for i in range(NCH):
            landed(rows(five, 0), sy.at[i])


def gather_and_multiply(p_tiles, tasks):
    dma = pltpu.SemaphoreType.DMA
    block = pltpu.VMEM((NT, TILE, TILE), jnp.float32)
    target = pltpu.VMEM((NC, TILE, TILE), jnp.float32)
    return pl.pallas_call(
        kernel,
        out_shape=jax.ShapeDtypeStruct((NC, TILE, TILE), jnp.float32),
        in_specs=[pl.BlockSpec(memory_space=pl.ANY), pl.BlockSpec(memory_space=pltpu.VMEM)],
        out_specs=pl.BlockSpec(memory_space=pltpu.VMEM),
        scratch_shapes=[block] * 15
        + [
            pltpu.VMEM((NTASK, TILE, TILE), jnp.float32),
            target,
            target,
            pltpu.VMEM((4, 8, 128), jnp.int32),
            pltpu.SMEM((2, 4, 8, 128), jnp.int32),
        ]
        + [dma((4,)), dma((12,)), dma((12,)), dma((12,)), dma((2, 3, 4)), dma((8,)), dma((4,)), dma((4,))] * 2
        + [dma, dma((4,)), dma((4,)), dma((2, 4)), pltpu.SemaphoreType.REGULAR, pltpu.VMEM((8, 8, 128), jnp.int32)],
        compiler_params=pltpu.CompilerParams(
            collective_id=0, has_side_effects=True, vmem_limit_bytes=60 * 1024 * 1024
        ),
    )(p_tiles, tasks)


def per_device(p_tiles, tasks):
    own = p_tiles.reshape(NT, TILE, TILE)
    return gather_and_multiply(own, jnp.transpose(tasks[0, 0], (1, 0, 2)))[None, None]


def solution(mesh):
    return jax.shard_map(
        per_device,
        mesh=mesh,
        in_specs=(P("blk", "rep", None, None, None, None), P("blk", "rep", None, None, None)),
        out_specs=P("blk", "rep", None, None, None),
        check_vma=False,
    )
```

```python
import jax
import jax.numpy as jnp
from jax import lax
from jax.experimental import pallas as pl
from jax.experimental.pallas import tpu as pltpu
from jax.sharding import PartitionSpec as P

MESH = pl.DeviceIdType.MESH
TILE = 128
NT = 40
TPS = 5
NC = 16
NTASK = 48
CH = 10
NCH = NT // CH
ORDER_OF_CHUNK = (0, 1, 3, 2)

WAIT_MATE, WAIT_PLUS, WAIT_MINUS, WAIT_CROSS, WAIT_Z = 0, 1, 2, 3, 4
LEFT_TO_MATE, TO_PLUS, TO_MINUS, TO_CROSS, TO_Z, LET_SIBLING_GO, PANEL_TO_MATE = 5, 6, 7, 8, 9, 10, 11
SCHEDULE = (
    (
        (804, 600, 700, 805, 601, 701, 900, 912, 901, 913, 902, 914, 903, 915, 806, 412, 400, 908, 0, 304, 413, 401,
         604, 704, 904, 916, 909, 807, 414, 402, 910, 1, 305, 415, 403, 605, 705, 917, 204, 104, 808, 416, 408, 920,
         905, 404, 417, 2, 306, 921, 606, 706, 919, 1000, 105, 205, 809, 420, 409, 500, 501, 502, 911, 503, 3, 307,
         607, 707, 918, 421, 410, 208, 106, 602, 702, 907, 308),
        (419, 405, 923, 206, 107, 810, 603, 703, 906, 309, 418, 411, 922, 207, 100, 811, 800, 608, 708),
        (310, 423, 407, 209, 101, 801, 609, 709),
        (311, 422, 406, 210, 102, 802, 610, 710, 300),
        (211, 103, 803, 611, 711, 301),
        (),
        (200, 108, 302, 201, 109, 303),
        (202, 110, 203, 111),
        (),
        (),
    ),
    (
        (804, 600, 805, 601, 900, 912, 901, 913, 902, 914, 903, 915, 806, 412, 400, 908, 100, 0, 304, 413, 401, 604,
         904, 916, 704, 909, 807, 414, 402, 910, 1, 101, 305, 415, 403, 605, 917, 705, 204, 708, 800, 416, 408, 920,
         905, 404, 417, 2, 104, 306, 921, 606, 919, 706, 1000, 205, 801, 420, 409, 500, 501, 502, 911, 503, 3, 105,
         307, 607, 918, 707, 421, 410, 208, 602, 802, 907, 709, 106, 300),
        (419, 405, 923, 206, 603, 803, 906, 710, 107, 301, 418, 411, 922, 207, 608),
        (711, 302, 102, 423, 407, 209, 609),
        (700, 303, 103, 422, 406, 210, 610, 701, 108),
        (211, 611, 702, 109),
        (),
        (200, 703, 110, 201, 111),
        (202, 203),
        (),
        (),
    ),
    (
        (804, 600, 805, 601, 900, 912, 901, 913, 902, 914, 903, 915, 806, 412, 400, 908, 100, 0, 304, 413, 401, 604,
         904, 916, 704, 909, 807, 414, 402, 910, 1, 101, 305, 415, 403, 605, 917, 705, 204, 708, 800, 416, 408, 920,
         905, 404, 417, 2, 306, 104, 921, 606, 919, 706, 1000, 205, 801, 420, 409, 500, 501, 502, 911, 503, 3, 105,
         307, 607, 918, 707, 421, 410, 206, 608, 802, 907, 709, 106, 300),
        (419, 405, 923, 207, 609, 803, 906, 710, 107, 301, 418, 411, 922, 208, 610),
        (711, 102, 302, 423, 407, 209, 611),
        (700, 303, 103, 422, 406, 210, 602, 701, 108),
        (211, 603, 702, 109),
        (),
        (200, 703, 110, 201, 111),
        (202, 203),
        (),
        (),
    ),
    (
        (804, 805, 900, 912, 901, 913, 902, 914, 903, 915, 806, 412, 400, 908, 200, 100, 0, 304, 413, 401, 904, 916,
         604, 704, 909, 807, 414, 402, 910, 1, 201, 101, 305, 415, 403, 917, 605, 705, 800, 416, 408, 920, 905, 404,
         417, 2, 204, 104, 306, 921, 919, 606, 706, 1000, 801, 420, 409, 500, 501, 502, 911, 708, 503, 3, 205, 307,
         105, 918, 607, 707, 421, 410, 802, 907, 709, 206, 106, 300, 600),
        (419, 405, 923, 803, 906, 710, 107, 207, 301, 601, 418, 411, 922, 808),
        (711, 108, 302, 202, 602, 423, 407, 809),
        (700, 109, 303, 203, 603, 422, 406, 810, 701, 110, 308, 208, 608),
        (811, 702, 111, 309, 209, 609),
        (),
        (703, 102, 310, 210, 610, 103, 311, 211, 611),
        (),
        (),
        (),
    ),
    (
        (1100, 1101, 1102, 1103, 900, 912, 901, 913, 902, 914, 0, 412, 400, 1, 903, 915, 2, 413, 401, 3, 904, 916,
         414, 402, 917, 908, 905, 918, 415, 403, 906, 919, 909, 416, 404, 920, 907, 408, 417, 921, 910, 405, 418, 922,
         911, 406, 419, 923, 409, 420),
        (407, 421),
        (410, 422),
        (411, 423),
        (),
        (),
        (),
        (),
        (),
        (),
    ),
)
HOLDER_TURNS = ((0, 1), (0, 0), (1, 1), (2, 1), (3, 1), None, (1, 0), (2, 0), (3, 0))
SIBLING_TURNS = ((0, 1), (1, 1), (2, 1), (3, 1), None, (0, 0), (1, 0), (2, 0), (3, 0))


MIDDLE = 8
FIRST_OF_SIBLING = next(op for segment in SCHEDULE[4] for op in segment if op // 100 == TO_Z)


def sort_tasks(tasks_ref, meta_ref):
    down = lax.broadcasted_iota(jnp.int32, (NTASK, NTASK), 0)
    along = lax.broadcasted_iota(jnp.int32, (NTASK, NTASK), 1)

    def turned(row):
        return jnp.sum(jnp.where(down == along, row, 0), axis=1, keepdims=True)

    for step in range(tasks_ref.shape[1]):
        row = lambda f: jnp.broadcast_to(tasks_ref[f, step : step + 1, :], (NTASK, NTASK))
        target = row(2)
        left, right, mine = turned(row(0)), turned(row(1)), turned(target)
        before = jnp.logical_or(target < mine, jnp.logical_and(target == mine, along < down))
        rank = jnp.sum(jnp.where(before, 1, 0), axis=1, keepdims=True)
        pick = lambda column, place: jnp.sum(jnp.where(rank == place, column, 0), axis=0, keepdims=True)
        here, ahead = pick(mine, along), pick(mine, along - 1)
        same = jnp.where(jnp.logical_and(here == ahead, along[:1] > 0), 1, 0)
        upto = jnp.sum(jnp.where(mine <= along, 1, 0), axis=0, keepdims=True)
        count = jnp.sum(jnp.where(mine == along, 1, 0), axis=0, keepdims=True)
        rows = (jnp.clip(pick(left, along), 0, NT - 1), jnp.clip(pick(right, along), 0, NT - 1), same)
        rows += (jnp.maximum(upto - 1, 0), jnp.where(count > 0, 1, 0))
        for f, v in enumerate(rows):
            meta_ref[step, f : f + 1, :NTASK] = v


def kernel(p_ref, tasks_ref, out_ref, *scratch):
    lefts = scratch[0:4]
    rights = (scratch[4:6], scratch[6:8], scratch[8:10], scratch[10:12])
    four = scratch[12:14]
    (five, sums, partial, arrived, meta_in, meta_sm) = scratch[14:20]
    (ry, rplus, rminus, rcross, rz, rd, rmeta, rc) = scratch[20:28]
    (sy, splus, sminus, scross, sz, sd, smeta, sc) = scratch[28:36]
    (l_own, l_left, l_part, l_meta, go, meta_ref) = scratch[36:42]

    blk, rep = lax.axis_index("blk"), lax.axis_index("rep")
    h, x, k = blk // 8, (blk % 8) // 2, blk % 2
    z, lo = rep // 2, rep % 2
    p = (lo + h) % 2
    holder = k == p
    mate = rep + 1 - 2 * lo
    at_plus = (h * 8 + ((x + 1) % 4) * 2 + k, rep)
    at_minus = (h * 8 + ((x + 3) % 4) * 2 + k, rep)
    at_mate = (blk, mate)
    at_cross = ((1 - h) * 8 + x * 2 + k, mate)
    at_zp = (blk, ((z + 1) % 4) * 2 + lo)
    at_zm = (blk, ((z + 3) % 4) * 2 + lo)
    at_sib = (blk + 1 - 2 * k, rep)

    def s_of(n, parity):
        odd = (k + parity) % 2
        f = (1 - k) * parity
        return odd + (0, 2, 6, 4)[n] + f * (0, 4, -2, -2)[n]

    barrier = pltpu.get_barrier_semaphore()
    for peer in (at_plus, at_minus, at_mate, at_cross, at_zp, at_zm, at_sib):
        pl.semaphore_signal(barrier, inc=1, device_id=peer, device_id_type=MESH)
    pl.semaphore_wait(barrier, 7)

    def remote(src, dst, ssem, rsem, peer):
        return pltpu.make_async_remote_copy(
            src_ref=src, dst_ref=dst, send_sem=ssem, recv_sem=rsem, device_id=peer, device_id_type=MESH
        )

    def rows(ref, i):
        return ref.at[pl.ds(CH * i, CH)]

    def five_of(ref, r):
        return ref.at[pl.ds(TPS * r, TPS)]

    def landed(ref, sem):
        pltpu.make_async_copy(ref, ref, sem).wait()

    def own(q, i):
        return rows(p_ref, i) if q == 0 else rows(rights[0][1], i)

    def to_sibling(here, src, n, q, i):
        @pl.when(here)
        def _():
            remote(src, rows(rights[n][q], i), sd.at[2 * n + q], rd.at[2 * n + q], at_sib).start()

    def sliver_of(side, kind):
        away = (z + 2) % 4 if kind == 2 else (z + 3) % 4 if side == 0 else (z + 1) % 4
        return away * 2 + (lo if kind == 0 or (kind == 2 and side == 0) else 1 - lo)

    def wait_z(side, kind, n):
        landed(five_of(lefts[n], sliver_of(side, kind)), rz.at[side, kind, n])

    def send_z(side, kind, n, held):
        if kind == 0:
            src, r = p_ref.at[pl.ds(TPS * s_of(n, p), TPS)], rep
        elif kind == 1:
            r = mate
            src = rights[0][1].at[pl.ds(CH * ORDER_OF_CHUNK[n], TPS)] if held else five_of(lefts[n], r)
        else:
            r = sliver_of(side, side)
            src = five_of(lefts[n], r)
        peer = (at_zp, at_zm)[side]
        remote(src, five_of(lefts[n], r), sz.at[side, kind, n], rz.at[side, kind, n], peer).start()

    def along_z(slot):
        return slot // 12, slot % 12 // 4, slot % 4

    def holder_op(op, x):
        what, slot = divmod(op, 100)
        if what == LET_SIBLING_GO:
            pl.semaphore_signal(go, inc=1, device_id=at_sib, device_id_type=MESH)
            return
        if what == WAIT_Z:
            wait_z(*along_z(slot))
            return
        if what == TO_Z:
            send_z(*along_z(slot), True)
            return
        q, i = slot // NCH, slot % NCH
        if what == LEFT_TO_MATE:
            src = p_ref.at[pl.ds(TPS * s_of(slot, 1 - p), TPS)]
            remote(src, five_of(lefts[slot], rep), sy.at[slot], ry.at[slot], at_mate).start()
        elif what == WAIT_MATE:
            src = rows(rights[0][1], i)
            landed(src, ry.at[i])
            n = ORDER_OF_CHUNK[i]
            head = rights[0][1].at[pl.ds(CH * i, TPS)]
            pltpu.make_async_copy(head, five_of(lefts[n], mate), l_part.at[n]).start()
            to_sibling(p == 0, src, 0, 1, i)
        elif what == WAIT_PLUS:
            n, f = (1, q) if q < 2 else (3, 1 if x == 3 else 0)
            src = rows(rights[n][f], i)
            landed(src, rplus.at[slot])
            if q < 2:
                to_sibling(p == 0, src, 1, q, i)
                to_sibling(p == 1, src, 0, q, i)
            else:
                to_sibling(p >= 0, src, 3, f, i)
        elif what == WAIT_MINUS:
            n, f = (2, q) if q < 2 else (3, 0 if x == 3 else 1)
            src = rows(rights[n][f], i)
            landed(src, rminus.at[slot])
            to_sibling(p >= 0, src, n, f, i)
        elif what == WAIT_CROSS:
            src = rows(four[q] if q < 2 else five, i)
            landed(src, rcross.at[slot])
            if q < 2:
                to_sibling(p == 1, src, 1, q, i)
        elif what == TO_PLUS:
            if q < 2:
                src, dst = rows(four[q], i) if x == 3 else own(q, i), rights[1][q]
            elif x == 3:
                src, dst = rows(five, i), rights[3][0]
            else:
                f = 1 if x == 2 else 0
                src, dst = rows(rights[1][f], i), rights[3][f]
            remote(src, rows(dst, i), splus.at[slot], rplus.at[slot], at_plus).start()
        elif what == TO_MINUS:
            if q < 2:
                src, dst = own(q, i) if x == 0 else rows(four[q], i), rights[2][q]
            elif x == 0:
                src, dst = rows(five, i), rights[3][0]
            else:
                src, dst = rows(rights[2][1], i), rights[3][1]
            remote(src, rows(dst, i), sminus.at[slot], rminus.at[slot], at_minus).start()
        else:
            if q < 2:
                src, dst = own(1 - q, i), four[q]
            else:
                src, dst = rows(rights[1][1] if x == 3 else rights[2][1], i), five
            remote(src, rows(dst, i), scross.at[slot], rcross.at[slot], at_cross).start()

    def sibling_op(op):
        what, slot = divmod(op, 100)
        if what == PANEL_TO_MATE:
            i = slot
            remote(rows(p_ref, i), rows(rights[0][1], i), sy.at[i], ry.at[i], at_mate).start()
        elif what == WAIT_MATE:
            landed(five_of(lefts[slot], mate), ry.at[slot])
        elif what == WAIT_Z:
            wait_z(*along_z(slot))
        else:
            if op == FIRST_OF_SIBLING:
                pl.semaphore_wait(go, 1)
            send_z(*along_z(slot), False)

    def keep_left():
        for n in range(4):
            src = p_ref.at[pl.ds(TPS * s_of(n, p), TPS)]
            pltpu.make_async_copy(src, five_of(lefts[n], rep), l_left.at[n]).start()

    def send_meta():
        for n in range(4):
            remote(meta_ref.at[s_of(n, 1 - p)], meta_in.at[n], smeta.at[n], rmeta.at[n], at_mate).start()
            pltpu.make_async_copy(meta_ref.at[s_of(n, p)], meta_sm.at[0, n], l_meta.at[0, n]).start()

    def on_meta():
        for n in range(4):
            landed(meta_in.at[n], rmeta.at[n])
            pltpu.make_async_copy(meta_in.at[n], meta_sm.at[1, n], l_meta.at[1, n]).start()
        for q in range(2):
            for n in range(4):
                landed(meta_sm.at[q, n], l_meta.at[q, n])

    def multiply(n, q):
        total = out_ref if q == 0 else partial

        def slot(j, acc):
            a = lefts[n][meta_sm[q, n, 0, j]]
            b = rights[n][q][meta_sm[q, n, 1, j]]
            a_hi = a.astype(jnp.bfloat16)
            a_lo = (a - a_hi.astype(jnp.float32)).astype(jnp.bfloat16)
            b_hi = b.astype(jnp.bfloat16)
            b_lo = (b - b_hi.astype(jnp.float32)).astype(jnp.bfloat16)
            both = jnp.dot(
                jnp.concatenate([a_hi, a_lo], axis=1),
                jnp.concatenate(
                    [jnp.concatenate([b_hi, b_hi], axis=0), jnp.concatenate([b_lo, jnp.zeros_like(b_lo)], axis=0)], axis=1
                ),
                preferred_element_type=jnp.float32,
            )
            prod = both[:, :TILE] + both[:, TILE:]
            acc = prod + jnp.where(meta_sm[q, n, 2, j] > 0, acc, 0.0)
            sums[j] = acc
            return acc

        lax.fori_loop(0, NTASK, slot, jnp.zeros((TILE, TILE), jnp.float32), unroll=16)

        def collect(c, carry):
            got = jnp.where(meta_sm[q, n, 4, c] > 0, sums[meta_sm[q, n, 3, c]], 0.0)
            if n == 0:
                total[c] = got
            else:
                total[c] += got
            return carry

        for g in range(4):
            lax.fori_loop(4 * g, 4 * g + 4, collect, 0)
            if (n, q) == (3, 1) and g > 0:
                send_sums(g - 1)

    def send_sums(g):
        part = pl.ds(4 * g, 4)
        remote(partial.at[part], arrived.at[part], sc.at[g], rc.at[g], at_mate).start()

    def turns(order, segment, held):
        ready = set()
        segment(0, None, 0)
        sort_tasks(tasks_ref, meta_ref)
        segment(0, 0, MIDDLE)
        send_meta()
        for step, turn in enumerate(order):
            segment(step, 0 if step else MIDDLE, None)
            if turn is None:
                send_sums(3)
                continue
            n, q = turn
            if not ready:
                on_meta()
            if n not in ready:
                ready.add(n)
                landed(five_of(lefts[n], rep), l_left.at[n])
                if held:
                    landed(five_of(lefts[n], mate), l_part.at[n])
            if not held:
                landed(rights[n][q], rd.at[2 * n + q])
            elif turn == (0, 0):
                landed(rights[0][0], l_own)
            multiply(n, q)
        segment(len(order), 0, None)
        for g in range(4):
            part = pl.ds(4 * g, 4)
            landed(arrived.at[part], rc.at[g])
            out_ref[part] += arrived[part]

    def part_of(c, step, begin, end):
        entries = SCHEDULE[c][step]
        first = 0
        if step == 0:
            first = next(i for i, op in enumerate(entries) if op // 100 <= WAIT_Z or (c == 4 and op // 100 == TO_Z))
        return entries[0 if begin is None else first + begin : None if end is None else first + end]

    @pl.when(holder)
    def _():
        def segment(step, begin, end):
            for c in range(4):
                ops = part_of(c, step, begin, end)
                if ops:

                    @pl.when(x == c)
                    def _():
                        for op in ops:
                            holder_op(op, c)

            if begin is None:
                keep_left()

                @pl.when(p == 0)
                def _():
                    remote(p_ref, rights[0][0], sd.at[0], rd.at[0], at_sib).start()

                pltpu.make_async_copy(p_ref, rights[0][0], l_own).start()

        turns(HOLDER_TURNS, segment, True)

    @pl.when(jnp.logical_not(holder))
    def _():
        def segment(step, begin, end):
            for op in part_of(4, step, begin, end):
                sibling_op(op)
            if begin is None:
                keep_left()

        turns(SIBLING_TURNS, segment, False)

    for n in range(4):
        landed(meta_in.at[n], smeta.at[n])
        landed(partial.at[pl.ds(4 * n, 4)], sc.at[n])
        for kind in range(3):
            for side in range(2):
                landed(five_of(lefts[n], 0), sz.at[side, kind, n])

    @pl.when(holder)
    def _():
        for i in range(NCH):
            landed(five_of(lefts[0], 0), sy.at[i])
        for slot in range(3 * NCH):
            landed(rows(five, 0), splus.at[slot])
            landed(rows(five, 0), sminus.at[slot])
        for slot in range(2 * NCH):
            landed(rows(five, 0), scross.at[slot])

        @pl.when(jnp.logical_or(x == 0, x == 3))
        def _():
            for i in range(NCH):
                landed(rows(five, 0), scross.at[2 * NCH + i])

        for b in range(8):
            landed(five, sd.at[b])

    @pl.when(jnp.logical_not(holder))
    def _():
        for i in range(NCH):
            landed(rows(five, 0), sy.at[i])


def gather_and_multiply(p_tiles, tasks):
    dma = pltpu.SemaphoreType.DMA
    block = pltpu.VMEM((NT, TILE, TILE), jnp.float32)
    target = pltpu.VMEM((NC, TILE, TILE), jnp.float32)
    return pl.pallas_call(
        kernel,
        out_shape=jax.ShapeDtypeStruct((NC, TILE, TILE), jnp.float32),
        in_specs=[pl.BlockSpec(memory_space=pl.ANY), pl.BlockSpec(memory_space=pltpu.VMEM)],
        out_specs=pl.BlockSpec(memory_space=pltpu.VMEM),
        scratch_shapes=[block] * 15
        + [
            pltpu.VMEM((NTASK, TILE, TILE), jnp.float32),
            target,
            target,
            pltpu.VMEM((4, 8, 128), jnp.int32),
            pltpu.SMEM((2, 4, 8, 128), jnp.int32),
        ]
        + [dma((4,)), dma((12,)), dma((12,)), dma((12,)), dma((2, 3, 4)), dma((8,)), dma((4,)), dma((4,))] * 2
        + [dma, dma((4,)), dma((4,)), dma((2, 4)), pltpu.SemaphoreType.REGULAR, pltpu.VMEM((8, 8, 128), jnp.int32)],
        compiler_params=pltpu.CompilerParams(
            collective_id=0, has_side_effects=True, vmem_limit_bytes=60 * 1024 * 1024
        ),
    )(p_tiles, tasks)


def per_device(p_tiles, tasks):
    own = p_tiles.reshape(NT, TILE, TILE)
    return gather_and_multiply(own, jnp.transpose(tasks[0, 0], (1, 0, 2)))[None, None]


def solution(mesh):
    return jax.shard_map(
        per_device,
        mesh=mesh,
        in_specs=(P("blk", "rep", None, None, None, None), P("blk", "rep", None, None, None)),
        out_specs=P("blk", "rep", None, None, None),
        check_vma=False,
    )
```
